128 devices in a mesh: group: 8 (over y, core), local: 16 (over z, x).
Axes of the slice: x: 4, y: 4, z: 4, core: 2. Of those that a mesh axis runs over, the one named last changes fastest.
Arguments:
- hidden_states: bfloat16 [16384, 3584], P(('group', 'local')), may hold values from -6 to 6
- affinity: float32 [16384, 8], P(('group', 'local')), may hold values from 0.1 to 1
- group_ids: int32 [16384, 4], P(('group', 'local')), may hold values from 0 to 7, as said below
- expert_ids: int32 [16384, 8], P(('group', 'local')), may hold values from 0 to 127, as said below
- w_gate: bfloat16 [128, 3584, 1024], P(('group', 'local')), may hold values from -0.09375 to 0.09375
- w_up: bfloat16 [128, 3584, 1024], P(('group', 'local')), may hold values from -0.09375 to 0.09375
- w_down: bfloat16 [128, 1024, 3584], P(('group', 'local')), may hold values from -0.1875 to 0.1875
Outputs:
- routed_out: bfloat16 [16384, 3584], P(('group', 'local'))
The draws below stay inside these ranges and needn't reach their ends.
Inputs may be any that keep to these rules, and one draw needn't show every extreme that they name: `group_ids`: each row names 4 different groups, and every group is named by exactly 64 of the tokens of one device. `expert_ids`: each row names 8 different experts; columns 2 j and 2 j + 1 lie in group group_ids[t, j]. Of the tokens of one device at most 10 name any one expert, and in every group some expert is named by exactly 10 tokens of every device.
All inputs are finite; a program needn't handle non-finite values.
Results may differ from the reference program's by a relative error of at most 0.007.
Values may be sent and summed in bfloat16 or wider, within the bound.
A program may use at most 128 MiB of HBM per device.

```python
import math
import jax
import jax.numpy as jnp
from jax import lax

D = 3584
HID = 1024
TOP_K = 8
TOPG = 4
TOK_DEV = 128
GROUPS = 8
EXP_GROUP = 16
EXPERTS = 128
TOKENS = 16384
TOK_GRP = 64
MOST = 10


def group_counts(count_key, hot_local):
    expert_rank = jax.random.permutation(jax.random.fold_in(count_key, 1), EXP_GROUP)
    move_sizes = jax.random.randint(jax.random.fold_in(count_key, 2), (EXP_GROUP,), 0, 4)
    positions = jnp.arange(EXP_GROUP)
    total_rest = 2 * TOK_GRP - MOST
    even_share = total_rest // (EXP_GROUP - 1)
    extra_count = total_rest % (EXP_GROUP - 1)
    base_by = even_share + (positions < extra_count).astype(jnp.int32)
    pair_first = positions // 2 * 2
    pair_second = jnp.minimum(pair_first + 1, EXP_GROUP - 1)
    paired = pair_first + 1 <= EXP_GROUP - 2
    step_size = jnp.minimum(move_sizes[positions // 2], jnp.minimum(MOST - base_by[pair_first], base_by[pair_second]))
    step_size = jnp.where(paired, step_size, 0)
    adjusted = base_by + jnp.where(positions % 2 == 0, step_size, -step_size)
    hot_rank = expert_rank[hot_local]
    dense_rank = expert_rank - (expert_rank > hot_rank).astype(jnp.int32)
    counts = adjusted[jnp.clip(dense_rank, 0, EXP_GROUP - 1)]
    return jnp.where(positions == hot_local, MOST, counts).astype(jnp.int32)


def device_routes(dev_key, hot_local):
    token_rank = jax.random.permutation(jax.random.fold_in(dev_key, 1), TOK_DEV)
    group_order = jax.random.permutation(jax.random.fold_in(dev_key, 2), GROUPS)
    count_keys = jax.vmap(lambda index_g: jax.random.fold_in(dev_key, 10 + index_g))(jnp.arange(GROUPS))
    counts = jax.vmap(group_counts)(count_keys, hot_local)
    bounds = jnp.cumsum(counts, axis=1)
    slots = jnp.arange(2 * TOK_GRP)
    expert_list = jnp.sum((bounds[:, None, :] <= slots[None, :, None]).astype(jnp.int32), axis=2)
    steps_j = jnp.arange(TOPG)
    chosen = group_order[(token_rank[:, None] + steps_j[None, :]) % GROUPS]
    within = token_rank[:, None] // GROUPS * TOPG + steps_j[None, :]
    first_local = expert_list[chosen, within]
    second_local = expert_list[chosen, within + TOK_GRP]
    experts = chosen[:, :, None] * EXP_GROUP + jnp.stack([first_local, second_local], axis=2)
    return (chosen.astype(jnp.int32), experts.reshape(TOK_DEV, TOP_K).astype(jnp.int32))


def route_tables(key):
    route_key = jax.random.fold_in(key, 4242)
    hot_local = jax.random.randint(jax.random.fold_in(route_key, 1), (GROUPS,), 0, EXP_GROUP)
    dev_keys = jax.vmap(lambda index_d: jax.random.fold_in(route_key, 100 + index_d))(jnp.arange(GROUPS * EXP_GROUP))
    chosen, experts = jax.vmap(lambda dev_key: device_routes(dev_key, hot_local))(dev_keys)
    return (chosen.reshape(TOKENS, TOPG), experts.reshape(TOKENS, TOP_K))


def draw_group_ids(key, part):
    return route_tables(key)[0]


def draw_expert_ids(key, part):
    return route_tables(key)[1]


def level_of(stream_key, dims, cuts, smallest, top_value):
    level = 1.0
    for axis_at, parts in cuts:
        draws = jax.random.uniform(jax.random.fold_in(jax.random.fold_in(stream_key, 6), axis_at), (parts,), jnp.float32, smallest / len(cuts), top_value / len(cuts))
        level = level * jnp.repeat(jnp.exp(draws), dims[axis_at] // parts).reshape((-1,) + (1,) * (len(dims) - 1 - axis_at))
    return level


def gaussian(rng, shape, width, most, split=(), kind=jnp.bfloat16):
    array = jax.random.normal(rng, shape, jnp.float32) * width
    if len(split) > 0:
        array = level_of(rng, shape, split, -0.22, 0.18) * array
    return jnp.clip(array, min=-most, max=most).astype(kind)


def setup_inputs(seed: int = 0) -> dict:
    key_list = jax.random.split(jax.random.key(seed), 8)
    return {
        "hidden_states": gaussian(key_list[0], (TOKENS, D), 1.0, 6.0, ((0, 128),)),
        "affinity": jnp.clip(jnp.exp(math.log(1.0) - 2.3025851 * jax.random.uniform(key_list[1], (TOKENS, TOP_K), jnp.float32) ** level_of(key_list[1], (TOKENS, TOP_K), ((0, 128),), -0.2, 0.2)), 0.1, 1.0),
        "group_ids": draw_group_ids(jax.random.fold_in(key_list[7], 71), 0),
        "expert_ids": draw_expert_ids(jax.random.fold_in(key_list[7], 71), 0),
        "w_gate": gaussian(key_list[4], (EXPERTS, D, HID), D ** -0.5, 0.09375, ((0, 128),)),
        "w_up": gaussian(key_list[5], (EXPERTS, D, HID), D ** -0.5, 0.09375, ((0, 128),)),
        "w_down": gaussian(key_list[6], (EXPERTS, HID, D), HID ** -0.5, 0.1875, ((0, 128),)),
    }


def expert_apply(rows_in, gate_mat, up_mat, down_mat):
    gate_act = jnp.dot(rows_in, gate_mat, preferred_element_type=jnp.float32)
    up_act = jnp.dot(rows_in, up_mat, preferred_element_type=jnp.float32)
    hidden = (jax.nn.silu(gate_act) * up_act).astype(jnp.bfloat16)
    return jnp.dot(hidden, down_mat, preferred_element_type=jnp.float32).astype(jnp.bfloat16)


def reference(hidden_states, affinity, group_ids, expert_ids, w_gate, w_up, w_down):
    gate_weights = (2.5 * affinity / jnp.sum(affinity, axis=1, keepdims=True)).astype(jnp.bfloat16)
    pair_size = TOP_K // TOPG
    chosen = jnp.repeat(group_ids, pair_size, axis=1)
    is_valid = (expert_ids // EXP_GROUP) == chosen
    mixing = jnp.where(is_valid, gate_weights, jnp.zeros((), jnp.bfloat16))
    flat_ids = jnp.where(is_valid, expert_ids, -1).reshape(-1)
    flat_total = TOKENS * TOP_K
    capacity = EXPERTS * MOST

    def one_expert(collected, inputs):
        expert, gate_mat, up_mat, down_mat = inputs
        found_at = jnp.nonzero(flat_ids == expert, size=capacity, fill_value=flat_total)[0].astype(jnp.int32)
        token_rows = hidden_states[jnp.minimum(found_at, flat_total - 1) // TOP_K]
        produced = expert_apply(token_rows, gate_mat, up_mat, down_mat)
        return collected.at[found_at].set(produced, mode="drop"), None

    scanned = lax.scan(one_expert, jnp.zeros((flat_total, D), jnp.bfloat16),
                       (jnp.arange(EXPERTS, dtype=jnp.int32), w_gate, w_up, w_down))
    outputs = scanned[0]
    blocks = TOKENS // TOK_DEV
    outs_b = outputs.reshape(blocks, TOK_DEV, TOPG, pair_size, D)
    mix_b = mixing.reshape(blocks, TOK_DEV, TOPG, pair_size)

    def combine(inputs):
        block_out, block_mix = inputs
        group_part = jnp.einsum("tgk,tgkd->tgd", block_mix.astype(jnp.float32), block_out.astype(jnp.float32)).astype(jnp.bfloat16)
        group_part = lax.optimization_barrier(group_part)
        return jnp.sum(group_part.astype(jnp.float32), axis=1).astype(jnp.bfloat16)

    mixed_rows = lax.map(combine, (outs_b, mix_b))
    return mixed_rows.reshape(TOKENS, D)
```

```python
import functools

import jax
import jax.numpy as jnp
from jax import lax
from jax.experimental import pallas as pl
from jax.experimental.pallas import tpu as pltpu
from jax.sharding import PartitionSpec as P

TOP_K = 8
TOPG = 4
SIDE = 4
MESH = pl.DeviceIdType.MESH
LAG_X = 1
LAG_C = 3
LAG_F = 5


def position():
    g = lax.axis_index("group")
    l = lax.axis_index("local")
    return g, l // SIDE, l % SIDE


def wait_bytes(ref, sem):
    pltpu.make_async_copy(ref, ref, sem).wait()


def group_peer(g, step, groups):
    return lax.rem(g + step, groups)


def ring_peer(p, step):
    return lax.rem(p + step, SIDE)


def entry_barrier(g, z, x, groups):
    bar = pltpu.get_barrier_semaphore()
    for step in range(1, groups):
        pl.semaphore_signal(
            bar, inc=1, device_id=(group_peer(g, step, groups), z * SIDE + x), device_id_type=MESH
        )
    for step in range(1, SIDE):
        pl.semaphore_signal(bar, inc=1, device_id=(g, ring_peer(z, step) * SIDE + x), device_id_type=MESH)
        pl.semaphore_signal(bar, inc=1, device_id=(g, z * SIDE + ring_peer(x, step)), device_id_type=MESH)
    pl.semaphore_wait(bar, groups - 1 + 2 * (SIDE - 1))


def send_groups(src, dst, chunk, g, z, x, groups, ssem, rsem):
    for step in range(1, groups):
        peer = group_peer(g, step, groups)
        pltpu.make_async_remote_copy(
            src_ref=src.at[chunk, peer],
            dst_ref=dst.at[chunk, g],
            send_sem=ssem,
            recv_sem=rsem.at[chunk],
            device_id=(peer, z * SIDE + x),
            device_id_type=MESH,
        ).start()


def send_z(src, dst, chunk, g, z, x, ssem, rsem):
    for step in (2, 1, 3):
        peer = ring_peer(z, step)
        pltpu.make_async_remote_copy(
            src_ref=src.at[chunk, peer],
            dst_ref=dst.at[chunk, z],
            send_sem=ssem,
            recv_sem=rsem.at[chunk],
            device_id=(g, peer * SIDE + x),
            device_id_type=MESH,
        ).start()
    dst[chunk, z] = src[chunk, z]


def send_x(src, dst, chunk, g, z, x, ssem, rsem):
    for step in (2, 1, 3):
        peer = ring_peer(x, step)
        pltpu.make_async_remote_copy(
            src_ref=src.at[chunk, :, peer],
            dst_ref=dst.at[chunk, :, x],
            send_sem=ssem,
            recv_sem=rsem.at[chunk],
            device_id=(g, z * SIDE + peer),
            device_id_type=MESH,
        ).start()
    for row in range(SIDE):
        dst[chunk, row, x] = src[chunk, row, x]


def dispatch_kernel(
    chunks, groups, slots,
    rt_ref, tok_ref, wg_ref, wu_ref,
    hid_ref, mix_ref, back_ref,
    meta_out, meta_in, first_out, first_in, out_buf, relay, rows,
    acc_g, acc_u, wbuf_g, wbuf_u, pick, sel,
    s_meta, r_meta, s_first, r_first, s_z, r_z, s_x, r_x, w_sem,
):
    g, z, x = position()
    tok = tok_ref.shape[0]
    width = tok_ref.shape[1] // chunks
    seats = tok * TOPG // groups
    held = groups * seats
    block = SIDE * slots
    total = SIDE * block

    def weights(c):
        slot = lax.rem(c, 2)
        start = pl.multiple_of(c * width, width)
        return (
            pltpu.make_async_copy(wg_ref.at[pl.ds(start, width)], wbuf_g.at[slot], w_sem.at[0, slot]),
            pltpu.make_async_copy(wu_ref.at[pl.ds(start, width)], wbuf_u.at[slot], w_sem.at[1, slot]),
        )

    for c in range(2):
        for cp in weights(c):
            cp.start()

    rt = rt_ref[...]
    rt_t = jnp.transpose(rt)
    group_at = lax.broadcasted_iota(jnp.int32, (groups, tok), 0).astype(jnp.float32)
    member = jnp.zeros((groups, tok), jnp.float32)
    for j in range(TOPG):
        member = member + (rt_t[2 * TOP_K + j : 2 * TOP_K + j + 1, :] == group_at).astype(jnp.float32)
    earlier = (
        lax.broadcasted_iota(jnp.int32, (tok, tok), 0) < lax.broadcasted_iota(jnp.int32, (tok, tok), 1)
    ).astype(jnp.bfloat16)
    before = jnp.dot(member.astype(jnp.bfloat16), earlier, preferred_element_type=jnp.float32)
    seat = jnp.where(member > 0, before, -1.0)
    seat_at = lax.broadcasted_iota(jnp.int32, (seats, tok), 0).astype(jnp.float32)
    for gg in range(groups):
        sel[gg * seats : (gg + 1) * seats, :] = (
            (seat_at == seat[gg : gg + 1, :]).astype(jnp.float32).astype(jnp.bfloat16)
        )
    meta = jnp.dot(sel[...], rt.astype(jnp.bfloat16), preferred_element_type=jnp.float32).astype(jnp.bfloat16)
    meta_out[0] = meta.reshape(groups, seats, 128)
    meta_in[0, g] = meta_out[0, g]

    entry_barrier(g, z, x, groups)
    send_groups(meta_out, meta_in, 0, g, z, x, groups, s_meta, r_meta)

    def first(c, carry):
        cols = pl.ds(pl.multiple_of(c * width, width), width)
        got = jnp.dot(sel[...], tok_ref[:, cols], preferred_element_type=jnp.float32).astype(jnp.bfloat16)
        first_out[c] = got.reshape(groups, seats, width)
        first_in[c, g] = first_out[c, g]
        send_groups(first_out, first_in, c, g, z, x, groups, s_first, r_first)
        return carry

    lax.fori_loop(0, chunks, first, 0)

    wait_bytes(meta_in.at[0, pl.ds(0, groups - 1)], r_meta.at[0])
    info = jnp.transpose(meta_in[0].reshape(held, 128).astype(jnp.float32))
    mine = g.astype(jnp.float32)
    ids = [jnp.zeros((1, held), jnp.float32) for _ in range(2)]
    mix = [jnp.zeros((1, held), jnp.float32) for _ in range(2)]
    for j in range(TOPG):
        here = info[2 * TOP_K + j : 2 * TOP_K + j + 1, :] == mine
        for k in range(2):
            ids[k] = ids[k] + jnp.where(here, info[2 * j + k : 2 * j + k + 1, :] + 1.0, 0.0)
            mix[k] = mix[k] + jnp.where(here, info[TOP_K + 2 * j + k : TOP_K + 2 * j + k + 1, :], 0.0)
    experts = SIDE * SIDE
    expert_at = lax.broadcasted_iota(jnp.int32, (experts, held), 0).astype(jnp.float32) + 1.0
    named = (ids[0] == expert_at).astype(jnp.float32) + (ids[1] == expert_at).astype(jnp.float32)
    earlier_row = (
        lax.broadcasted_iota(jnp.int32, (held, held), 0) < lax.broadcasted_iota(jnp.int32, (held, held), 1)
    ).astype(jnp.bfloat16)
    ahead = jnp.dot(named.astype(jnp.bfloat16), earlier_row, preferred_element_type=jnp.float32)
    place = []
    for k in range(2):
        rank = jnp.sum(jnp.where(ids[k] == expert_at, ahead, 0.0), axis=0, keepdims=True)
        place.append(jnp.where(ids[k] > 0, (ids[k] - 1.0) * slots + rank, -1.0))
    row_at = lax.broadcasted_iota(jnp.int32, (block, held), 0).astype(jnp.float32)
    for zz in range(SIDE):
        base = row_at + float(zz * block)
        pick[zz * block : (zz + 1) * block, :] = (
            ((base == place[0]).astype(jnp.float32) + (base == place[1]).astype(jnp.float32)).astype(jnp.bfloat16)
        )

    def step(i, carry):
        @pl.when(i < chunks)
        def _():
            wait_bytes(first_in.at[i, pl.ds(0, groups - 1)], r_first.at[i])
            src = first_in[i].reshape(held, width)
            for zz in range(SIDE):
                got = jnp.dot(
                    pick[zz * block : (zz + 1) * block, :], src, preferred_element_type=jnp.float32
                ).astype(jnp.bfloat16)
                out_buf[i, zz] = got.reshape(SIDE, slots, width)
            send_z(out_buf, relay, i, g, z, x, s_z, r_z)

        @pl.when((i >= LAG_X) & (i < chunks + LAG_X))
        def _():
            c = i - LAG_X
            wait_bytes(relay.at[c, pl.ds(0, SIDE - 1)], r_z.at[c])
            send_x(relay, rows, c, g, z, x, s_x, r_x)

        @pl.when(i == LAG_C)
        def _():
            cols = jnp.concatenate(
                [place[0], place[1], mix[0], mix[1], jnp.zeros((124, held), jnp.float32)], axis=0
            )
            cols = jnp.transpose(cols)
            slot_at = lax.broadcasted_iota(jnp.int32, (held, total), 1).astype(jnp.float32)
            mix_ref[...] = (
                jnp.where(slot_at == cols[:, 0:1], cols[:, 2:3], 0.0)
                + jnp.where(slot_at == cols[:, 1:2], cols[:, 3:4], 0.0)
            ).astype(jnp.bfloat16)
            seat_t = jnp.transpose(
                jnp.concatenate([seat, jnp.full((tok - groups, tok), -1.0, jnp.float32)], axis=0)
            )
            lane = lax.broadcasted_iota(jnp.int32, (tok, held), 1)
            lane_at = lane.astype(jnp.float32)
            back = jnp.zeros((tok, held), jnp.float32)
            for gg in range(groups):
                column = seat_t[:, gg : gg + 1]
                want = jnp.where(column >= 0, column + float(gg * seats), -1.0)
                back = back + (lane_at == want).astype(jnp.float32)
            back_ref[...] = back.astype(jnp.bfloat16)

        @pl.when(i >= LAG_C)
        def _():
            c = i - LAG_C
            slot = lax.rem(c, 2)
            wait_bytes(rows.at[c, pl.ds(0, SIDE - 1)], r_x.at[c])
            for cp in weights(c):
                cp.wait()

            def piece(zz, inner):
                at = pl.ds(pl.multiple_of(zz * block, block), block)
                part = rows[c, zz].reshape(block, width)
                got_g = jnp.dot(part, wbuf_g[slot], preferred_element_type=jnp.float32)
                got_u = jnp.dot(part, wbuf_u[slot], preferred_element_type=jnp.float32)

                @pl.when(c == 0)
                def _():
                    acc_g[at, :] = got_g
                    acc_u[at, :] = got_u

                @pl.when(c > 0)
                def _():
                    acc_g[at, :] = acc_g[at, :] + got_g
                    acc_u[at, :] = acc_u[at, :] + got_u

                return inner

            lax.fori_loop(0, SIDE, piece, 0)

            @pl.when(c + 2 < chunks)
            def _():
                for cp in weights(c + 2):
                    cp.start()

        return carry

    lax.fori_loop(0, chunks + LAG_C, step, 0)

    def finish(b, carry):
        at = pl.ds(pl.multiple_of(b * slots, slots), slots)
        v = acc_g[at, :]
        hid_ref[at, :] = (v / (1.0 + jnp.exp(-v)) * acc_u[at, :]).astype(jnp.bfloat16)
        return carry

    lax.fori_loop(0, total // slots, finish, 0)
    wait_bytes(meta_out.at[0, pl.ds(0, groups - 1)], s_meta)
    wait_bytes(first_out.at[:, pl.ds(0, groups - 1)], s_first)
    wait_bytes(out_buf.at[:, pl.ds(0, SIDE - 1)], s_z)
    wait_bytes(relay.at[:, pl.ds(0, SIDE - 1)], s_x)


def return_kernel(
    chunks, groups, slots,
    hid_ref, mix_ref, back_ref, wd_ref,
    out_ref,
    out_buf, relay, rows, part_out, part_in, wbuf,
    s_z, r_z, s_x, r_x, s_last, r_last, w_sem,
):
    g, z, x = position()
    width = out_ref.shape[1] // chunks
    held = mix_ref.shape[0]
    seats = held // groups
    block = SIDE * slots
    total = SIDE * block

    def weights(c):
        slot = lax.rem(c, 2)
        start = pl.multiple_of(c * width, width)
        return pltpu.make_async_copy(wd_ref.at[:, pl.ds(start, width)], wbuf.at[slot], w_sem.at[slot])

    for c in range(2):
        weights(c).start()
    entry_barrier(g, z, x, groups)

    def step(i, carry):
        @pl.when(i < chunks)
        def _():
            weights(i).wait()
            slot = lax.rem(i, 2)

            def piece(zz, inner):
                at = pl.ds(pl.multiple_of(zz * block, block), block)
                got = jnp.dot(hid_ref[at, :], wbuf[slot], preferred_element_type=jnp.float32).astype(jnp.bfloat16)
                out_buf[i, zz] = got.reshape(SIDE, slots, width)
                return inner

            lax.fori_loop(0, SIDE, piece, 0)
            send_z(out_buf, relay, i, g, z, x, s_z, r_z)

            @pl.when(i + 2 < chunks)
            def _():
                weights(i + 2).start()

        @pl.when((i >= LAG_X) & (i < chunks + LAG_X))
        def _():
            c = i - LAG_X
            wait_bytes(relay.at[c, pl.ds(0, SIDE - 1)], r_z.at[c])
            send_x(relay, rows, c, g, z, x, s_x, r_x)

        @pl.when((i >= LAG_C) & (i < chunks + LAG_C))
        def _():
            c = i - LAG_C
            wait_bytes(rows.at[c, pl.ds(0, SIDE - 1)], r_x.at[c])
            got = jnp.dot(
                mix_ref[...], rows[c].reshape(total, width), preferred_element_type=jnp.float32
            ).astype(jnp.bfloat16)
            part_out[c] = got.reshape(groups, seats, width)
            send_groups(part_out, part_in, c, g, z, x, groups, s_last, r_last)
            part_in[c, g] = part_out[c, g]

        @pl.when(i >= LAG_F)
        def _():
            c = i - LAG_F
            wait_bytes(part_in.at[c, pl.ds(0, groups - 1)], r_last.at[c])
            out_ref[:, pl.ds(pl.multiple_of(c * width, width), width)] = jnp.dot(
                back_ref[...], part_in[c].reshape(held, width), preferred_element_type=jnp.float32
            ).astype(jnp.bfloat16)

        return carry

    lax.fori_loop(0, chunks + LAG_F, step, 0)
    wait_bytes(out_buf.at[:, pl.ds(0, SIDE - 1)], s_z)
    wait_bytes(relay.at[:, pl.ds(0, SIDE - 1)], s_x)
    wait_bytes(part_out.at[:, pl.ds(0, groups - 1)], s_last)


def shards(hidden_states, affinity, group_ids, expert_ids, w_gate, w_up, w_down):
    tok, model = hidden_states.shape
    hid = w_gate.shape[2]
    groups = lax.axis_size("group")
    local = lax.axis_size("local")
    most = 5 * tok * TOP_K // (4 * groups * local)
    slots = most * groups
    seats = tok * TOPG // groups
    held = groups * seats
    total = local * slots
    chunks = 14
    width = model // chunks
    pair = TOP_K // TOPG

    weights = (2.5 * affinity / jnp.sum(affinity, axis=1, keepdims=True)).astype(jnp.bfloat16)
    is_valid = expert_ids // local == jnp.repeat(group_ids, pair, axis=1)
    mixing = jnp.where(is_valid, weights, jnp.zeros((), jnp.bfloat16)).astype(jnp.float32)
    inside = jnp.where(is_valid, expert_ids % local, -1).astype(jnp.float32)
    rt = jnp.concatenate(
        [inside, mixing, group_ids.astype(jnp.float32), jnp.zeros((tok, 128 - 2 * TOP_K - TOPG), jnp.float32)],
        axis=1,
    )

    vmem = pl.BlockSpec(memory_space=pltpu.VMEM)
    anywhere = pl.BlockSpec(memory_space=pl.ANY)
    bf16 = jnp.bfloat16
    dma = pltpu.SemaphoreType.DMA
    hidden, mix, back = pl.pallas_call(
        functools.partial(dispatch_kernel, chunks, groups, slots),
        out_shape=(
            jax.ShapeDtypeStruct((total, hid), bf16),
            jax.ShapeDtypeStruct((held, total), bf16),
            jax.ShapeDtypeStruct((tok, held), bf16),
        ),
        in_specs=[vmem, vmem, anywhere, anywhere],
        out_specs=(vmem, vmem, vmem),
        scratch_shapes=[
            pltpu.VMEM((1, groups, seats, 128), bf16),
            pltpu.VMEM((1, groups, seats, 128), bf16),
            pltpu.VMEM((chunks, groups, seats, width), bf16),
            pltpu.VMEM((chunks, groups, seats, width), bf16),
            pltpu.VMEM((chunks, SIDE, SIDE, slots, width), bf16),
            pltpu.VMEM((chunks, SIDE, SIDE, slots, width), bf16),
            pltpu.VMEM((chunks, SIDE, SIDE, slots, width), bf16),
            pltpu.VMEM((total, hid), jnp.float32),
            pltpu.VMEM((total, hid), jnp.float32),
            pltpu.VMEM((2, width, hid), bf16),
            pltpu.VMEM((2, width, hid), bf16),
            pltpu.VMEM((total, held), bf16),
            pltpu.VMEM((held, tok), bf16),
            dma, dma((1,)), dma, dma((chunks,)), dma, dma((chunks,)), dma, dma((chunks,)), dma((2, 2)),
        ],
        compiler_params=pltpu.CompilerParams(
            collective_id=0, has_side_effects=True, vmem_limit_bytes=60 * 2**20
        ),
        name="dispatch",
    )(rt, hidden_states, w_gate[0], w_up[0])

    return pl.pallas_call(
        functools.partial(return_kernel, chunks, groups, slots),
        out_shape=jax.ShapeDtypeStruct((tok, model), bf16),
        in_specs=[vmem, vmem, vmem, anywhere],
        out_specs=vmem,
        scratch_shapes=[
            pltpu.VMEM((chunks, SIDE, SIDE, slots, width), bf16),
            pltpu.VMEM((chunks, SIDE, SIDE, slots, width), bf16),
            pltpu.VMEM((chunks, SIDE, SIDE, slots, width), bf16),
            pltpu.VMEM((chunks, groups, seats, width), bf16),
            pltpu.VMEM((chunks, groups, seats, width), bf16),
            pltpu.VMEM((2, hid, width), bf16),
            dma, dma((chunks,)), dma, dma((chunks,)), dma, dma((chunks,)), dma((2,)),
        ],
        compiler_params=pltpu.CompilerParams(
            collective_id=1, has_side_effects=True, vmem_limit_bytes=60 * 2**20
        ),
        name="giveback",
    )(hidden, mix, back, w_down[0])


def solution(mesh):
    placed = (
        P(("group", "local"), None),
        P(("group", "local"), None),
        P(("group", "local"), None),
        P(("group", "local"), None),
        P(("group", "local"), None, None),
        P(("group", "local"), None, None),
        P(("group", "local"), None, None),
    )
    return jax.shard_map(
        shards, mesh=mesh, in_specs=placed, out_specs=P(("group", "local"), None), check_vma=False
    )
```

```python
import functools

import jax
import jax.numpy as jnp
from jax import lax
from jax.experimental import pallas as pl
from jax.experimental.pallas import tpu as pltpu
from jax.sharding import PartitionSpec as P

TOP_K = 8
TOPG = 4
SIDE = 4
MOST = 10
CHUNKS = 14
N_G = 5
N_X = 5
N_Z = 4
LANES = 128
MESH = pl.DeviceIdType.MESH
BF16 = jnp.bfloat16
F32 = jnp.float32


def position():
    g = lax.axis_index("group")
    l = lax.axis_index("local")
    return g, l // SIDE, l % SIDE


def wait_bytes(ref, sem):
    pltpu.make_async_copy(ref, ref, sem).wait()


def ring(p, step):
    return lax.rem(p + step, SIDE)


def remote(src, dst, ssem, rsem, g, z, x):
    pltpu.make_async_remote_copy(
        src_ref=src, dst_ref=dst, send_sem=ssem, recv_sem=rsem, device_id=(g, z * SIDE + x), device_id_type=MESH
    ).start()


def iota(shape, axis):
    return lax.broadcasted_iota(jnp.int32, shape, axis).astype(F32)


def one_hot(mask):
    return jnp.where(mask, 1.0, 0.0).astype(BF16)


def dot(a, b):
    return jnp.dot(a, b, preferred_element_type=F32)


def signal_peers(sem, g, z, x, groups):
    for step in range(1, groups):
        pl.semaphore_signal(
            sem, inc=1, device_id=(lax.rem(g + step, groups), z * SIDE + x), device_id_type=MESH
        )
    for step in range(1, SIDE):
        pl.semaphore_signal(sem, inc=1, device_id=(g, ring(z, step) * SIDE + x), device_id_type=MESH)
        pl.semaphore_signal(sem, inc=1, device_id=(g, z * SIDE + ring(x, step)), device_id_type=MESH)


def entry_barrier(g, z, x, groups):
    bar = pltpu.get_barrier_semaphore()
    signal_peers(bar, g, z, x, groups)
    pl.semaphore_wait(bar, groups - 1 + 2 * (SIDE - 1))


def send_groups(src, dst, c, g, z, x, groups, ssem, rsem):
    for step in range(1, groups):
        peer = lax.rem(g + step, groups)
        remote(src.at[c, peer], dst.at[c, g], ssem, rsem, peer, z, x)
    dst[c, g] = src[c, g]


def send_pairs(src, dst, c, g, z, x, groups, ssem, rsem):
    for step in range(1, groups):
        peer = lax.rem(g + step, groups)
        remote(src.at[c, pl.ds(2 * peer, 2)], dst.at[c, pl.ds(2 * g, 2)], ssem, rsem, peer, z, x)
    dst[c, pl.ds(2 * g, 2)] = src[c, pl.ds(2 * g, 2)]


def along_z(src, sc, dst, dc, g, z, x, ssem, rsem):
    for step in (2, 1, 3):
        peer = ring(z, step)
        remote(src.at[sc, peer], dst.at[dc, z], ssem, rsem, g, peer, x)
    dst[dc, z] = src[sc, z]


def along_x(src, sc, dst, dc, g, z, x, ssem, rsem):
    for step in (2, 1, 3):
        peer = ring(x, step)
        remote(src.at[sc, :, peer], dst.at[dc, :, x], ssem, rsem, g, z, peer)
    for row in range(SIDE):
        dst[dc, row, x] = src[sc, row, x]


def rank_table(eids, mixes, experts, span):
    rows, cols = experts.shape
    named = jnp.zeros((rows, cols), F32)
    weight = jnp.zeros((rows, cols), F32)
    for k in range(TOP_K):
        hit = eids[k] == experts
        named = named + jnp.where(hit, 1.0, 0.0)
        weight = weight + jnp.where(hit, mixes[k], 0.0)
    r = iota((cols, cols), 0)
    c = iota((cols, cols), 1)
    earlier = one_hot((r < c) & (jnp.floor(r / span) == jnp.floor(c / span)))
    ahead = dot(named.astype(BF16), earlier)
    return jnp.where(named > 0, ahead, -1.0), weight


def fill_pick(pick, seat, per_expert, blocks, span):
    total, cols = pick.shape
    rows = seat.shape[0]
    part = total // SIDE
    seat16 = seat.astype(BF16)
    column = 16.0 * jnp.floor(iota((part, cols), 1) / span)
    for p in range(SIDE):
        at = iota((part, rows), 0) + float(p * part)
        spread = one_hot(jnp.floor((at + 0.5) / per_expert) == iota((part, rows), 1))
        slot = iota((part, 1), 0) + float(p * part)
        ten = jnp.floor((slot + 0.5) / MOST)
        code = (slot - MOST * ten) + 16.0 * (ten - blocks * jnp.floor((ten + 0.5) / blocks))
        pick[p * part : (p + 1) * part, :] = one_hot(dot(spread, seat16) + column == code)


def fill_mix(mix, seat, weight, per_expert, blocks, span):
    cols, total = mix.shape
    rows = seat.shape[0]
    both = jnp.concatenate([seat, weight, jnp.zeros((LANES - 2 * rows, cols), F32)], axis=0)
    turned = jnp.transpose(both).astype(BF16)
    owner = jnp.floor((iota((LANES, total), 1) + 0.5) / per_expert)
    lane = iota((LANES, total), 0)
    spread_seat = one_hot(owner == lane)
    spread_mix = one_hot(owner + float(rows) == lane)
    slot = iota((1, total), 1)
    ten = jnp.floor((slot + 0.5) / MOST)
    code = (slot - MOST * ten) + 16.0 * (ten - blocks * jnp.floor((ten + 0.5) / blocks))
    part = cols // SIDE
    for p in range(SIDE):
        here = turned[p * part : (p + 1) * part, :]
        row = 16.0 * jnp.floor((iota((part, 1), 0) + float(p * part)) / span)
        mix[p * part : (p + 1) * part, :] = jnp.where(
            dot(here, spread_seat) + row == code, dot(here, spread_mix), 0.0
        ).astype(BF16)


def fill_swap(swap, outer, inner):
    total = swap.shape[0]
    part = total // SIDE
    lane = iota((part, total), 1)
    for p in range(SIDE):
        slot = iota((part, 1), 0) + float(p * part)
        ten = jnp.floor((slot + 0.5) / MOST)
        o = jnp.floor((ten + 0.5) / inner)
        i = ten - o * inner
        swap[p * part : (p + 1) * part, :] = one_hot(lane == (i * outer + o) * MOST + (slot - MOST * ten))


def read_info(info):
    ids = []
    mixes = []
    for k in range(TOP_K):
        inside = info[k : k + 1, :]
        group = info[2 * TOP_K + k // 2 : 2 * TOP_K + k // 2 + 1, :]
        ids.append(jnp.where(inside >= 0, inside + float(SIDE * SIDE) * group, -1.0))
        mixes.append(info[TOP_K + k : TOP_K + k + 1, :])
    return ids, mixes


def dispatch_kernel(
    groups, slots,
    aff_ref, gid_ref, eid_ref, tok_ref, wg_ref, wu_ref,
    hid_ref, mix_g, mix_x, mix_z, back_ref,
    info_out, info_x, info_z, meta_out, meta_in, first_out, first_in, wide_x, wide_z,
    out_g, relay_g, y_out, y_in, rows, acc_g, acc_u, wbuf_g, wbuf_u, pick_g, pick_x, pick_z, swap, sel, stage,
    s_info, r_info, s_meta, r_meta, s_first, r_first, s_wide_x, s_wide_z, r_wide, s_one, r_one,
    s_two, s_y, r_y, s_end, r_rows, w_sem, mix_sem,
):
    g, z, x = position()
    tok = tok_ref.shape[0]
    width = tok_ref.shape[1] // CHUNKS
    seats = tok * TOPG // groups
    held = groups * seats
    block = SIDE * slots
    total = SIDE * block
    local = SIDE * SIDE

    def columns(c):
        return pl.ds(pl.multiple_of(c * width, width), width)

    def weights(c):
        slot = lax.rem(c, 2)
        return (
            pltpu.make_async_copy(wg_ref.at[columns(c)], wbuf_g.at[slot], w_sem.at[0, slot]),
            pltpu.make_async_copy(wu_ref.at[columns(c)], wbuf_u.at[slot], w_sem.at[1, slot]),
        )

    for c in range(2):
        for cp in weights(c):
            cp.start()

    aff = aff_ref[...]
    scaled = (2.5 * aff / jnp.sum(aff, axis=1, keepdims=True)).astype(BF16)
    gid = gid_ref[...].astype(F32)
    eid = eid_ref[...].astype(F32)
    twice = one_hot(jnp.floor(iota((TOPG, TOP_K), 1) / 2.0) == iota((TOPG, TOP_K), 0))
    chosen = dot(gid.astype(BF16), twice)
    owner = jnp.floor(eid / float(local))
    is_valid = owner == chosen
    mixing = jnp.where(is_valid, scaled.astype(F32), 0.0).astype(BF16)
    inside = jnp.where(is_valid, eid - float(local) * owner, -1.0).astype(BF16)
    lane_of = iota((TOP_K, LANES), 1) - iota((TOP_K, LANES), 0)
    lane_of4 = iota((TOPG, LANES), 1) - iota((TOPG, LANES), 0)
    rt = (
        dot(inside, one_hot(lane_of == 0.0))
        + dot(mixing, one_hot(lane_of == float(TOP_K)))
        + dot(gid.astype(BF16), one_hot(lane_of4 == float(2 * TOP_K)))
    )
    info_out[...] = rt.astype(BF16)
    info_x[x] = info_out[...]
    info_z[z] = info_out[...]

    entry_barrier(g, z, x, groups)
    for step in (2, 1, 3):
        peer = ring(x, step)
        remote(info_out, info_x.at[x], s_info.at[0], r_info.at[0], g, z, peer)
        peer = ring(z, step)
        remote(info_out, info_z.at[z], s_info.at[1], r_info.at[1], g, peer, x)

    rt_t = jnp.transpose(rt)
    group_at = iota((groups, tok), 0)
    member = jnp.zeros((groups, tok), F32)
    for j in range(TOPG):
        member = member + jnp.where(rt_t[2 * TOP_K + j : 2 * TOP_K + j + 1, :] == group_at, 1.0, 0.0)
    earlier = one_hot(iota((tok, tok), 0) < iota((tok, tok), 1))
    seat = jnp.where(member > 0, dot(member.astype(BF16), earlier), -1.0)
    seat_at = iota((seats, tok), 0)
    for gg in range(groups):
        sel[gg * seats : (gg + 1) * seats, :] = one_hot(seat_at == seat[gg : gg + 1, :])
    meta_out[0] = dot(sel[...], info_out[...]).astype(BF16).reshape(groups, seats, LANES)
    send_groups(meta_out, meta_in, 0, g, z, x, groups, s_meta, r_meta)

    def first(t, carry):
        got = dot(sel[...], tok_ref[:, columns(3 * t)]).astype(BF16)
        first_out[t] = got.reshape(groups, seats, width)
        send_groups(first_out, first_in, t, g, z, x, groups, s_first, r_first.at[t])
        wide_x[t, x] = tok_ref[:, columns(3 * t + 1)]
        for step in (2, 1, 3):
            remote(wide_x.at[t, x], wide_x.at[t, x], s_wide_x, r_wide.at[t], g, z, ring(x, step))

        @pl.when(t < N_Z)
        def _():
            wide_z[t, z] = tok_ref[:, columns(3 * t + 2)]
            for step in (2, 1, 3):
                remote(wide_z.at[t, z], wide_z.at[t, z], s_wide_z, r_wide.at[N_X + t], g, ring(z, step), x)

        return carry

    lax.fori_loop(0, N_G, first, 0)

    row = iota((2 * local, held), 0)
    wait_bytes(info_x.at[pl.ds(0, SIDE - 1)], r_info.at[0])
    ids, mixes = read_info(jnp.transpose(info_x[...].reshape(held, LANES).astype(F32)))
    seat_x, weight_x = rank_table(ids, mixes, row * float(SIDE) + x.astype(F32), float(tok))
    fill_pick(pick_x, seat_x, float(SIDE * MOST), float(SIDE), float(tok))
    wait_bytes(meta_in.at[0, pl.ds(0, groups - 1)], r_meta)
    ids, mixes = read_info(jnp.transpose(meta_in[0].reshape(held, LANES).astype(F32)))
    seat_g, weight_g = rank_table(
        ids, mixes, iota((local, held), 0) + float(local) * g.astype(F32), float(seats)
    )
    fill_pick(pick_g, seat_g, float(slots), float(groups), float(seats))
    wait_bytes(info_z.at[pl.ds(0, SIDE - 1)], r_info.at[1])
    ids, mixes = read_info(jnp.transpose(info_z[...].reshape(held, LANES).astype(F32)))
    own = jnp.floor(row / float(SIDE)) * float(local - SIDE) + row + float(SIDE) * z.astype(F32)
    seat_z, weight_z = rank_table(ids, mixes, own, float(tok))
    fill_pick(pick_z, seat_z, float(SIDE * MOST), float(SIDE), float(tok))

    def to_peers(c, src, pick):
        for p in range(SIDE):
            got = dot(pick[p * block : (p + 1) * block, :], src).astype(BF16)
            y_out[c, pl.ds(p * SIDE, SIDE)] = got.reshape(SIDE, slots, width)
        send_pairs(y_out, y_in, c, g, z, x, groups, s_y.at[c], r_y.at[c])

    def reorder(c):
        wait_bytes(y_in.at[c, pl.ds(0, 2 * groups - 2)], r_y.at[c])
        wait_bytes(y_out.at[c, pl.ds(0, 2 * groups - 2)], s_y.at[c])
        src = y_in[c].reshape(total, width)
        for p in range(SIDE):
            got = dot(swap[p * block : (p + 1) * block, :], src).astype(BF16)
            y_out[c, pl.ds(p * SIDE, SIDE)] = got.reshape(SIDE, slots, width)

    def step(t, carry):
        @pl.when(t < N_G)
        def _():
            wait_bytes(first_in.at[t, pl.ds(0, groups - 1)], r_first.at[t])
            src = first_in[t].reshape(held, width)
            for p in range(SIDE):
                got = dot(pick_g[p * block : (p + 1) * block, :], src).astype(BF16)
                out_g[t, p] = got.reshape(SIDE, slots, width)

            @pl.when(lax.rem(t, 2) == 0)
            def _():
                along_x(out_g, t, relay_g, t, g, z, x, s_one, r_one.at[t])

            @pl.when(lax.rem(t, 2) == 1)
            def _():
                along_z(out_g, t, relay_g, t, g, z, x, s_one, r_one.at[t])

        @pl.when(t < N_X)
        def _():
            wait_bytes(wide_x.at[t, pl.ds(0, SIDE - 1)], r_wide.at[t])
            to_peers(t, wide_x[t].reshape(held, width), pick_x)

        @pl.when(t < N_Z)
        def _():
            wait_bytes(wide_z.at[t, pl.ds(0, SIDE - 1)], r_wide.at[N_X + t])
            to_peers(N_X + t, wide_z[t].reshape(held, width), pick_z)

        @pl.when(t == 0)
        def _():
            fill_swap(swap, local, groups)

        @pl.when((t >= 1) & (t < N_G + 1))
        def _():
            c = t - 1
            wait_bytes(relay_g.at[c, pl.ds(0, SIDE - 1)], r_one.at[c])

            @pl.when(lax.rem(c, 2) == 0)
            def _():
                along_z(relay_g, c, rows, 3 * c, g, z, x, s_two, r_rows.at[3 * c])

            @pl.when(lax.rem(c, 2) == 1)
            def _():
                along_x(relay_g, c, rows, 3 * c, g, z, x, s_two, r_rows.at[3 * c])

        @pl.when((t >= 1) & (t < N_X + 1))
        def _():
            c = t - 1
            reorder(c)
            for step in (2, 1, 3):
                peer = ring(z, step)
                remote(
                    y_out.at[c, pl.ds(SIDE * peer, SIDE)], rows.at[3 * c + 1, z], s_end, r_rows.at[3 * c + 1],
                    g, peer, x,
                )
            rows[3 * c + 1, z] = y_out[c, pl.ds(SIDE * z, SIDE)]

        @pl.when((t >= 1) & (t < N_Z + 1))
        def _():
            c = t - 1
            reorder(N_X + c)
            for step in (2, 1, 3):
                peer = ring(x, step)
                remote(
                    y_out.at[N_X + c, pl.ds(SIDE * peer, SIDE)], rows.at[3 * c + 2, :, x], s_end,
                    r_rows.at[3 * c + 2], g, z, peer,
                )
            for p in range(SIDE):
                rows[3 * c + 2, p, x] = y_out[N_X + c, SIDE * x + p]

        @pl.when(t == 1)
        def _():
            def keep(mix):
                put = pltpu.make_async_copy(stage, mix, mix_sem)
                put.start()
                put.wait()

            fill_mix(stage, seat_g, weight_g, float(slots), float(groups), float(seats))
            keep(mix_g)
            fill_mix(stage, seat_x, weight_x, float(SIDE * MOST), float(SIDE), float(tok))
            keep(mix_x)
            fill_mix(stage, seat_z, weight_z, float(SIDE * MOST), float(SIDE), float(tok))
            keep(mix_z)
            seat_t = jnp.transpose(jnp.concatenate([seat, jnp.full((tok - groups, tok), -1.0, F32)], axis=0))
            lane_at = iota((tok, held), 1)
            back = jnp.zeros((tok, held), F32)
            for gg in range(groups):
                column = seat_t[:, gg : gg + 1]
                want = jnp.where(column >= 0, column + float(gg * seats), -1.0)
                back = back + jnp.where(lane_at == want, 1.0, 0.0)
            back_ref[...] = back.astype(BF16)

        def multiply(c, carry_in):
            slot = lax.rem(c, 2)
            wait_bytes(rows.at[c, pl.ds(0, SIDE - 1)], r_rows.at[c])
            for cp in weights(c):
                cp.wait()

            def piece(p, inner):
                at = pl.ds(pl.multiple_of(p * block, block), block)
                part = rows[c, p].reshape(block, width)
                got_g = dot(part, wbuf_g[slot])
                got_u = dot(part, wbuf_u[slot])

                @pl.when(c == 0)
                def _():
                    acc_g[at, :] = got_g
                    acc_u[at, :] = got_u

                @pl.when(c > 0)
                def _():
                    acc_g[at, :] = acc_g[at, :] + got_g
                    acc_u[at, :] = acc_u[at, :] + got_u

                return inner

            lax.fori_loop(0, SIDE, piece, 0)

            @pl.when(c + 2 < CHUNKS)
            def _():
                for cp in weights(c + 2):
                    cp.start()

            return carry_in

        @pl.when(t >= 2)
        def _():
            low = 3 * (t - 2)
            lax.fori_loop(low, jnp.minimum(low + 3, CHUNKS), multiply, 0)

        return carry

    lax.fori_loop(0, N_G + 2, step, 0)

    def finish(b, carry):
        at = pl.ds(pl.multiple_of(b * slots, slots), slots)
        v = acc_g[at, :]
        hid_ref[at, :] = (v / (1.0 + jnp.exp(-v)) * acc_u[at, :]).astype(BF16)
        return carry

    lax.fori_loop(0, total // slots, finish, 0)
    wait_bytes(info_x.at[pl.ds(0, SIDE - 1)], s_info.at[0])
    wait_bytes(info_z.at[pl.ds(0, SIDE - 1)], s_info.at[1])
    wait_bytes(meta_out.at[0, pl.ds(0, groups - 1)], s_meta)
    wait_bytes(first_out.at[:, pl.ds(0, groups - 1)], s_first)
    wait_bytes(wide_x.at[:, pl.ds(0, SIDE - 1)], s_wide_x)
    wait_bytes(wide_z.at[:, pl.ds(0, SIDE - 1)], s_wide_z)
    wait_bytes(out_g.at[:, pl.ds(0, SIDE - 1)], s_one)
    wait_bytes(relay_g.at[:, pl.ds(0, SIDE - 1)], s_two)
    wait_bytes(y_out.at[:, pl.ds(0, SIDE * (SIDE - 1))], s_end)


def return_kernel(
    groups, slots,
    hid_ref, mix_g, mix_x, mix_z, back_ref, wd_ref,
    out_ref,
    out_buf, relay_g, rows_g, mid, y_out, y_in, part_out, part_in, sum_out, sum_in, wbuf, swap,
    s_one, r_one, s_two, r_two, s_mid, r_mid, s_y, r_y, s_last, r_last, s_sum_x, s_sum_z, r_sum, w_sem,
):
    g, z, x = position()
    tok = out_ref.shape[0]
    width = out_ref.shape[1] // CHUNKS
    held = mix_g.shape[0]
    seats = held // groups
    block = SIDE * slots
    total = SIDE * block

    def columns(c):
        return pl.ds(pl.multiple_of(c * width, width), width)

    def weights(c):
        slot = lax.rem(c, 2)
        return pltpu.make_async_copy(wd_ref.at[:, columns(c)], wbuf.at[slot], w_sem.at[slot])

    for c in range(2):
        weights(c).start()
    entry_barrier(g, z, x, groups)

    def down(c):
        slot = lax.rem(c, 2)
        weights(c).wait()

        def piece(p, inner):
            at = pl.ds(pl.multiple_of(p * block, block), block)
            got = dot(hid_ref[at, :], wbuf[slot]).astype(BF16)
            out_buf[c, p] = got.reshape(SIDE, slots, width)
            return inner

        lax.fori_loop(0, SIDE, piece, 0)

        @pl.when(c + 2 < CHUNKS)
        def _():
            weights(c + 2).start()

    def to_sources(c):
        wait_bytes(mid.at[c, pl.ds(0, SIDE * (SIDE - 1))], r_mid.at[c])
        src = mid[c].reshape(total, width)
        for p in range(SIDE):
            got = dot(swap[p * block : (p + 1) * block, :], src).astype(BF16)
            y_out[c, pl.ds(p * SIDE, SIDE)] = got.reshape(SIDE, slots, width)
        send_pairs(y_out, y_in, c, g, z, x, groups, s_y, r_y.at[c])

    def weigh(c, mix):
        wait_bytes(y_in.at[c, pl.ds(0, 2 * groups - 2)], r_y.at[c])
        got = dot(mix[...], y_in[c].reshape(total, width)).astype(BF16)
        sum_out[c] = got.reshape(SIDE, tok, width)

    def add_up(c):
        wait_bytes(sum_in.at[c, pl.ds(0, SIDE - 1)], r_sum.at[c])
        got = sum_in[c, 0].astype(F32)
        for b in range(1, SIDE):
            got = got + sum_in[c, b].astype(F32)
        return got.astype(BF16)

    def step(t, carry):
        @pl.when(t < N_G)
        def _():
            down(3 * t)

            @pl.when(lax.rem(t, 2) == 0)
            def _():
                along_x(out_buf, 3 * t, relay_g, t, g, z, x, s_one, r_one.at[t])

            @pl.when(lax.rem(t, 2) == 1)
            def _():
                along_z(out_buf, 3 * t, relay_g, t, g, z, x, s_one, r_one.at[t])

        @pl.when(t < N_X)
        def _():
            c = 3 * t + 1
            down(c)
            for step in (2, 1, 3):
                peer = ring(z, step)
                remote(out_buf.at[c, peer], mid.at[t, pl.ds(SIDE * z, SIDE)], s_mid.at[0], r_mid.at[t], g, peer, x)
            mid[t, pl.ds(SIDE * z, SIDE)] = out_buf[c, z]

        @pl.when(t < N_Z)
        def _():
            c = 3 * t + 2
            down(c)
            for step in (2, 1, 3):
                peer = ring(x, step)
                remote(
                    out_buf.at[c, :, peer], mid.at[N_X + t, pl.ds(SIDE * x, SIDE)], s_mid.at[1],
                    r_mid.at[N_X + t], g, z, peer,
                )
            for p in range(SIDE):
                mid[N_X + t, SIDE * x + p] = out_buf[c, p, x]

        @pl.when(t == 0)
        def _():
            fill_swap(swap, groups, SIDE * SIDE)

        @pl.when((t >= 1) & (t < N_G + 1))
        def _():
            c = t - 1
            wait_bytes(relay_g.at[c, pl.ds(0, SIDE - 1)], r_one.at[c])

            @pl.when(lax.rem(c, 2) == 0)
            def _():
                along_z(relay_g, c, rows_g, c, g, z, x, s_two, r_two.at[c])

            @pl.when(lax.rem(c, 2) == 1)
            def _():
                along_x(relay_g, c, rows_g, c, g, z, x, s_two, r_two.at[c])

        @pl.when((t >= 1) & (t < N_X + 1))
        def _():
            to_sources(t - 1)

        @pl.when((t >= 1) & (t < N_Z + 1))
        def _():
            to_sources(N_X + t - 1)

        @pl.when((t >= 2) & (t < N_G + 2))
        def _():
            c = t - 2
            wait_bytes(rows_g.at[c, pl.ds(0, SIDE - 1)], r_two.at[c])
            got = dot(mix_g[...], rows_g[c].reshape(total, width)).astype(BF16)
            part_out[c] = got.reshape(groups, seats, width)
            send_groups(part_out, part_in, c, g, z, x, groups, s_last, r_last.at[c])

        @pl.when((t >= 2) & (t < N_X + 2))
        def _():
            c = t - 2
            weigh(c, mix_x)
            for step in (2, 1, 3):
                peer = ring(x, step)
                remote(sum_out.at[c, peer], sum_in.at[c, x], s_sum_x, r_sum.at[c], g, z, peer)
            sum_in[c, x] = sum_out[c, x]

        @pl.when((t >= 2) & (t < N_Z + 2))
        def _():
            c = N_X + t - 2
            weigh(c, mix_z)
            for step in (2, 1, 3):
                peer = ring(z, step)
                remote(sum_out.at[c, peer], sum_in.at[c, z], s_sum_z, r_sum.at[c], g, peer, x)
            sum_in[c, z] = sum_out[c, z]

        @pl.when((t >= 3) & (t < N_G + 3))
        def _():
            c = t - 3
            wait_bytes(part_in.at[c, pl.ds(0, groups - 1)], r_last.at[c])
            out_ref[:, columns(3 * c)] = dot(back_ref[...], part_in[c].reshape(held, width)).astype(BF16)

        @pl.when((t >= 3) & (t < N_X + 3))
        def _():
            out_ref[:, columns(3 * (t - 3) + 1)] = add_up(t - 3)

        @pl.when((t >= 3) & (t < N_Z + 3))
        def _():
            out_ref[:, columns(3 * (t - 3) + 2)] = add_up(N_X + t - 3)

        return carry

    lax.fori_loop(0, N_G + 3, step, 0)
    wait_bytes(relay_g.at[:, pl.ds(0, SIDE - 1)], s_one)
    wait_bytes(rows_g.at[:, pl.ds(0, SIDE - 1)], s_two)
    wait_bytes(mid.at[pl.ds(0, N_X), pl.ds(0, SIDE * (SIDE - 1))], s_mid.at[0])
    wait_bytes(mid.at[pl.ds(N_X, N_Z), pl.ds(0, SIDE * (SIDE - 1))], s_mid.at[1])
    wait_bytes(y_out.at[:, pl.ds(0, 2 * groups - 2)], s_y)
    wait_bytes(part_out.at[:, pl.ds(0, groups - 1)], s_last)
    wait_bytes(sum_out.at[pl.ds(0, N_X), pl.ds(0, SIDE - 1)], s_sum_x)
    wait_bytes(sum_out.at[pl.ds(N_X, N_Z), pl.ds(0, SIDE - 1)], s_sum_z)


def shards(hidden_states, affinity, group_ids, expert_ids, w_gate, w_up, w_down):
    tok, model = hidden_states.shape
    hid = w_gate.shape[2]
    groups = lax.axis_size("group")
    slots = MOST * groups
    seats = tok * TOPG // groups
    held = groups * seats
    total = SIDE * SIDE * slots
    width = model // CHUNKS
    wide = N_X + N_Z

    vmem = pl.BlockSpec(memory_space=pltpu.VMEM)
    anywhere = pl.BlockSpec(memory_space=pl.ANY)
    dma = pltpu.SemaphoreType.DMA

    def grid4(n):
        return pltpu.VMEM((n, SIDE, SIDE, slots, width), BF16)

    def pairs(n):
        return pltpu.VMEM((n, SIDE * SIDE, slots, width), BF16)

    def seated(n, w):
        return pltpu.VMEM((n, groups, seats, w), BF16)

    def spread(n):
        return pltpu.VMEM((n, SIDE, tok, width), BF16)

    mix_shape = jax.ShapeDtypeStruct((held, total), BF16)
    hidden, mix_g, mix_x, mix_z, back = pl.pallas_call(
        functools.partial(dispatch_kernel, groups, slots),
        out_shape=(
            jax.ShapeDtypeStruct((total, hid), BF16), mix_shape, mix_shape, mix_shape,
            jax.ShapeDtypeStruct((tok, held), BF16),
        ),
        in_specs=[vmem, vmem, vmem, vmem, anywhere, anywhere],
        out_specs=(vmem, anywhere, anywhere, anywhere, vmem),
        scratch_shapes=[
            pltpu.VMEM((tok, LANES), BF16),
            pltpu.VMEM((SIDE, tok, LANES), BF16),
            pltpu.VMEM((SIDE, tok, LANES), BF16),
            seated(1, LANES), seated(1, LANES),
            seated(N_G, width), seated(N_G, width),
            spread(N_X), spread(N_Z),
            grid4(N_G), grid4(N_G),
            pairs(wide), pairs(wide),
            grid4(CHUNKS),
            pltpu.VMEM((total, hid), F32),
            pltpu.VMEM((total, hid), F32),
            pltpu.VMEM((2, width, hid), BF16),
            pltpu.VMEM((2, width, hid), BF16),
            pltpu.VMEM((total, held), BF16),
            pltpu.VMEM((total, held), BF16),
            pltpu.VMEM((total, held), BF16),
            pltpu.VMEM((total, total), BF16),
            pltpu.VMEM((held, tok), BF16),
            pltpu.VMEM((held, total), BF16),
            dma((2,)), dma((2,)), dma, dma, dma, dma((N_G,)), dma, dma, dma((wide,)), dma, dma((N_G,)),
            dma, dma((wide,)), dma((wide,)), dma, dma((CHUNKS,)), dma((2, 2)), dma,
        ],
        compiler_params=pltpu.CompilerParams(
            collective_id=0, has_side_effects=True, vmem_limit_bytes=63 * 2**20
        ),
        name="dispatch",
    )(affinity, group_ids, expert_ids, hidden_states, w_gate[0], w_up[0])

    return pl.pallas_call(
        functools.partial(return_kernel, groups, slots),
        out_shape=jax.ShapeDtypeStruct((tok, model), BF16),
        in_specs=[vmem, vmem, vmem, vmem, vmem, anywhere],
        out_specs=vmem,
        scratch_shapes=[
            grid4(CHUNKS), grid4(N_G), grid4(N_G),
            pairs(wide), pairs(wide), pairs(wide),
            seated(N_G, width), seated(N_G, width),
            spread(wide), spread(wide),
            pltpu.VMEM((2, hid, width), BF16),
            pltpu.VMEM((total, total), BF16),
            dma, dma((N_G,)), dma, dma((N_G,)), dma((2,)), dma((wide,)), dma, dma((wide,)),
            dma, dma((N_G,)), dma, dma, dma((wide,)), dma((2,)),
        ],
        compiler_params=pltpu.CompilerParams(
            collective_id=1, has_side_effects=True, vmem_limit_bytes=60 * 2**20
        ),
        name="giveback",
    )(hidden, mix_g, mix_x, mix_z, back, w_down[0])


def solution(mesh):
    placed = (
        P(("group", "local"), None),
        P(("group", "local"), None),
        P(("group", "local"), None),
        P(("group", "local"), None),
        P(("group", "local"), None, None),
        P(("group", "local"), None, None),
        P(("group", "local"), None, None),
    )
    return jax.shard_map(
        shards, mesh=mesh, in_specs=placed, out_specs=P(("group", "local"), None), check_vma=False
    )
```

```python
import functools

import jax
import jax.numpy as jnp
from jax import lax
from jax.experimental import pallas as pl
from jax.experimental.pallas import tpu as pltpu
from jax.sharding import PartitionSpec as P

TOP_K = 8
TOPG = 4
SIDE = 4
MOST = 10
CHUNKS = 14
N_G = 5
N_X = 5
N_Z = 4
LANES = 128
MESH = pl.DeviceIdType.MESH
BF16 = jnp.bfloat16
F32 = jnp.float32


def position():
    g = lax.axis_index("group")
    l = lax.axis_index("local")
    return g, l // SIDE, l % SIDE


def wait_bytes(ref, sem):
    pltpu.make_async_copy(ref, ref, sem).wait()


def ring(p, step):
    return lax.rem(p + step, SIDE)


def remote(src, dst, ssem, rsem, g, z, x):
    pltpu.make_async_remote_copy(
        src_ref=src, dst_ref=dst, send_sem=ssem, recv_sem=rsem, device_id=(g, z * SIDE + x), device_id_type=MESH
    ).start()


def iota(shape, axis):
    return lax.broadcasted_iota(jnp.int32, shape, axis).astype(F32)


def one_hot(mask):
    return jnp.where(mask, 1.0, 0.0).astype(BF16)


def dot(a, b):
    return jnp.dot(a, b, preferred_element_type=F32)


def signal_peers(sem, g, z, x, groups):
    for step in range(1, groups):
        pl.semaphore_signal(
            sem, inc=1, device_id=(lax.rem(g + step, groups), z * SIDE + x), device_id_type=MESH
        )
    for step in range(1, SIDE):
        pl.semaphore_signal(sem, inc=1, device_id=(g, ring(z, step) * SIDE + x), device_id_type=MESH)
        pl.semaphore_signal(sem, inc=1, device_id=(g, z * SIDE + ring(x, step)), device_id_type=MESH)


def entry_barrier(g, z, x, groups):
    bar = pltpu.get_barrier_semaphore()
    signal_peers(bar, g, z, x, groups)
    pl.semaphore_wait(bar, groups - 1 + 2 * (SIDE - 1))


def send_groups(src, dst, c, g, z, x, groups, ssem, rsem):
    for step in range(1, groups):
        peer = lax.rem(g + step, groups)
        remote(src.at[c, peer], dst.at[c, g], ssem, rsem, peer, z, x)
    dst[c, g] = src[c, g]


def send_pairs(src, dst, c, g, z, x, groups, ssem, rsem):
    for step in range(1, groups):
        peer = lax.rem(g + step, groups)
        remote(src.at[c, pl.ds(2 * peer, 2)], dst.at[c, pl.ds(2 * g, 2)], ssem, rsem, peer, z, x)
    dst[c, pl.ds(2 * g, 2)] = src[c, pl.ds(2 * g, 2)]


def along_z(src, sc, dst, dc, g, z, x, ssem, rsem):
    for step in (2, 1, 3):
        peer = ring(z, step)
        remote(src.at[sc, peer], dst.at[dc, z], ssem, rsem, g, peer, x)
    dst[dc, z] = src[sc, z]


def along_x(src, sc, dst, dc, g, z, x, ssem, rsem):
    for step in (2, 1, 3):
        peer = ring(x, step)
        remote(src.at[sc, :, peer], dst.at[dc, :, x], ssem, rsem, g, z, peer)
    for row in range(SIDE):
        dst[dc, row, x] = src[sc, row, x]


def rank_table(eids, mixes, experts, span):
    rows, cols = experts.shape
    named = jnp.zeros((rows, cols), F32)
    weight = jnp.zeros((rows, cols), F32)
    for k in range(TOP_K):
        hit = eids[k] == experts
        named = named + jnp.where(hit, 1.0, 0.0)
        weight = weight + jnp.where(hit, mixes[k], 0.0)
    r = iota((cols, cols), 0)
    c = iota((cols, cols), 1)
    earlier = one_hot((r < c) & (jnp.floor(r / span) == jnp.floor(c / span)))
    ahead = dot(named.astype(BF16), earlier)
    return jnp.where(named > 0, ahead, -1.0), weight


def fill_pick(pick, seat, per_expert, blocks, span):
    total, cols = pick.shape
    rows = seat.shape[0]
    part = total // SIDE
    seat16 = seat.astype(BF16)
    column = 16.0 * jnp.floor(iota((part, cols), 1) / span)
    for p in range(SIDE):
        at = iota((part, rows), 0) + float(p * part)
        spread = one_hot(jnp.floor((at + 0.5) / per_expert) == iota((part, rows), 1))
        slot = iota((part, 1), 0) + float(p * part)
        ten = jnp.floor((slot + 0.5) / MOST)
        code = (slot - MOST * ten) + 16.0 * (ten - blocks * jnp.floor((ten + 0.5) / blocks))
        pick[p * part : (p + 1) * part, :] = one_hot(dot(spread, seat16) + column == code)


def fill_mix(mix, seat, weight, per_expert, blocks, span):
    cols, total = mix.shape
    rows = seat.shape[0]
    both = jnp.concatenate([seat, weight, jnp.zeros((LANES - 2 * rows, cols), F32)], axis=0)
    turned = jnp.transpose(both).astype(BF16)
    owner = jnp.floor((iota((LANES, total), 1) + 0.5) / per_expert)
    lane = iota((LANES, total), 0)
    spread_seat = one_hot(owner == lane)
    spread_mix = one_hot(owner + float(rows) == lane)
    slot = iota((1, total), 1)
    ten = jnp.floor((slot + 0.5) / MOST)
    code = (slot - MOST * ten) + 16.0 * (ten - blocks * jnp.floor((ten + 0.5) / blocks))
    part = cols // SIDE
    for p in range(SIDE):
        here = turned[p * part : (p + 1) * part, :]
        row = 16.0 * jnp.floor((iota((part, 1), 0) + float(p * part)) / span)
        mix[p * part : (p + 1) * part, :] = jnp.where(
            dot(here, spread_seat) + row == code, dot(here, spread_mix), 0.0
        ).astype(BF16)


def fill_swap(swap, outer, inner):
    total = swap.shape[0]
    part = total // SIDE
    lane = iota((part, total), 1)
    for p in range(SIDE):
        slot = iota((part, 1), 0) + float(p * part)
        ten = jnp.floor((slot + 0.5) / MOST)
        o = jnp.floor((ten + 0.5) / inner)
        i = ten - o * inner
        swap[p * part : (p + 1) * part, :] = one_hot(lane == (i * outer + o) * MOST + (slot - MOST * ten))


def read_info(info):
    ids = []
    mixes = []
    for k in range(TOP_K):
        inside = info[k : k + 1, :]
        group = info[2 * TOP_K + k // 2 : 2 * TOP_K + k // 2 + 1, :]
        ids.append(jnp.where(inside >= 0, inside + float(SIDE * SIDE) * group, -1.0))
        mixes.append(info[TOP_K + k : TOP_K + k + 1, :])
    return ids, mixes


def dispatch_kernel(
    groups, slots,
    aff_ref, gid_ref, eid_ref, tok_ref, wg_ref, wu_ref,
    hid_ref, mix_g, mix_x, mix_z, back_ref,
    info_out, info_x, info_z, meta_out, meta_in, first_out, first_in, wide_x, wide_z,
    out_g, relay_g, y_out, y_in, rows, acc_g, acc_u, wbuf_g, wbuf_u, pick_g, pick_x, pick_z, swap, sel, stage, table,
    s_info, r_info, s_meta, r_meta, s_first, r_first, s_wide_x, s_wide_z, r_wide, s_one, r_one,
    s_two, s_y, r_y, s_end, r_rows, w_sem, mix_sem,
):
    g, z, x = position()
    tok = tok_ref.shape[0]
    width = tok_ref.shape[1] // CHUNKS
    seats = tok * TOPG // groups
    held = groups * seats
    block = SIDE * slots
    total = SIDE * block
    local = SIDE * SIDE

    def columns(c):
        return pl.ds(pl.multiple_of(c * width, width), width)

    def weights(c):
        slot = lax.rem(c, 2)
        return (
            pltpu.make_async_copy(wg_ref.at[columns(c)], wbuf_g.at[slot], w_sem.at[0, slot]),
            pltpu.make_async_copy(wu_ref.at[columns(c)], wbuf_u.at[slot], w_sem.at[1, slot]),
        )

    for c in range(2):
        for cp in weights(c):
            cp.start()

    aff = aff_ref[...]
    scaled = (2.5 * aff / jnp.sum(aff, axis=0, keepdims=True)).astype(BF16).astype(F32)
    gid = gid_ref[...].astype(F32)
    eid = eid_ref[...].astype(F32)
    owner = jnp.floor(eid / float(local))
    chosen = jnp.concatenate([gid[k // 2 : k // 2 + 1, :] for k in range(TOP_K)], axis=0)
    is_valid = owner == chosen
    mixing = jnp.where(is_valid, scaled, 0.0)
    inside = jnp.where(is_valid, eid - float(local) * owner, -1.0)
    rt_t = jnp.concatenate(
        [inside, mixing, gid, jnp.zeros((LANES - 2 * TOP_K - TOPG, tok), F32)], axis=0
    )
    rt = jnp.transpose(rt_t)
    info_out[...] = rt.astype(BF16)
    info_x[x] = info_out[...]
    info_z[z] = info_out[...]

    entry_barrier(g, z, x, groups)
    for step in (2, 1, 3):
        peer = ring(x, step)
        remote(info_out, info_x.at[x], s_info.at[0], r_info.at[0], g, z, peer)
        peer = ring(z, step)
        remote(info_out, info_z.at[z], s_info.at[1], r_info.at[1], g, peer, x)

    group_at = iota((groups, tok), 0)
    member = jnp.zeros((groups, tok), F32)
    for j in range(TOPG):
        member = member + jnp.where(rt_t[2 * TOP_K + j : 2 * TOP_K + j + 1, :] == group_at, 1.0, 0.0)
    earlier = one_hot(iota((tok, tok), 0) < iota((tok, tok), 1))
    seat = jnp.where(member > 0, dot(member.astype(BF16), earlier), -1.0)
    seat_at = iota((seats, tok), 0)
    for gg in range(groups):
        sel[gg * seats : (gg + 1) * seats, :] = one_hot(seat_at == seat[gg : gg + 1, :])
    meta_out[0] = dot(sel[...], info_out[...]).astype(BF16).reshape(groups, seats, LANES)
    send_groups(meta_out, meta_in, 0, g, z, x, groups, s_meta, r_meta)

    def first(t, carry):
        got = dot(sel[...], tok_ref[:, columns(3 * t)]).astype(BF16)
        first_out[t] = got.reshape(groups, seats, width)
        send_groups(first_out, first_in, t, g, z, x, groups, s_first, r_first.at[t])
        wide_x[t, x] = tok_ref[:, columns(3 * t + 1)]
        for step in (2, 1, 3):
            remote(wide_x.at[t, x], wide_x.at[t, x], s_wide_x, r_wide.at[t], g, z, ring(x, step))

        @pl.when(t < N_Z)
        def _():
            wide_z[t, z] = tok_ref[:, columns(3 * t + 2)]
            for step in (2, 1, 3):
                remote(wide_z.at[t, z], wide_z.at[t, z], s_wide_z, r_wide.at[N_X + t], g, ring(z, step), x)

        return carry

    lax.fori_loop(0, N_G, first, 0)

    def clear(b, carry):
        at = pl.ds(pl.multiple_of(b * slots, slots), slots)
        acc_g[at, :] = jnp.zeros((slots, acc_g.shape[1]), F32)
        acc_u[at, :] = jnp.zeros((slots, acc_u.shape[1]), F32)
        return carry

    lax.fori_loop(0, total // slots, clear, 0)

    def plan_g():
        wait_bytes(meta_in.at[0, pl.ds(0, groups - 1)], r_meta)
        ids, mixes = read_info(jnp.transpose(meta_in[0].reshape(held, LANES).astype(F32)))
        own = iota((local, held), 0) + float(local) * g.astype(F32)
        seat_in, weight = rank_table(ids, mixes, own, float(seats))
        fill_pick(pick_g, seat_in, float(slots), float(groups), float(seats))
        table[0, 0:local, :] = seat_in
        table[0, local : 2 * local, :] = weight

    def plan_wide(info, which, own, pick):
        wait_bytes(info.at[pl.ds(0, SIDE - 1)], r_info.at[which])
        ids, mixes = read_info(jnp.transpose(info[...].reshape(held, LANES).astype(F32)))
        seat_in, weight = rank_table(ids, mixes, own, float(tok))
        fill_pick(pick, seat_in, float(SIDE * MOST), float(SIDE), float(tok))
        table[1 + which, 0 : 2 * local, :] = seat_in
        table[1 + which, 2 * local : 4 * local, :] = weight

    def plan_x():
        plan_wide(info_x, 0, iota((2 * local, held), 0) * float(SIDE) + x.astype(F32), pick_x)

    def plan_z():
        row = iota((2 * local, held), 0)
        own = jnp.floor(row / float(SIDE)) * float(local - SIDE) + row + float(SIDE) * z.astype(F32)
        plan_wide(info_z, 1, own, pick_z)

    plan_g()

    def to_peers(c, src, pick):
        for p in range(SIDE):
            got = dot(pick[p * block : (p + 1) * block, :], src).astype(BF16)
            y_out[c, pl.ds(p * SIDE, SIDE)] = got.reshape(SIDE, slots, width)
        send_pairs(y_out, y_in, c, g, z, x, groups, s_y.at[c], r_y.at[c])

    def reorder(c):
        wait_bytes(y_in.at[c, pl.ds(0, 2 * groups - 2)], r_y.at[c])
        wait_bytes(y_out.at[c, pl.ds(0, 2 * groups - 2)], s_y.at[c])
        src = y_in[c].reshape(total, width)
        for p in range(SIDE):
            got = dot(swap[p * block : (p + 1) * block, :], src).astype(BF16)
            y_out[c, pl.ds(p * SIDE, SIDE)] = got.reshape(SIDE, slots, width)

    def step(t, carry):
        @pl.when(t < N_G)
        def _():
            wait_bytes(first_in.at[t, pl.ds(0, groups - 1)], r_first.at[t])
            src = first_in[t].reshape(held, width)
            for p in range(SIDE):
                got = dot(pick_g[p * block : (p + 1) * block, :], src).astype(BF16)
                out_g[t, p] = got.reshape(SIDE, slots, width)

            @pl.when(lax.rem(t, 2) == 0)
            def _():
                along_x(out_g, t, relay_g, t, g, z, x, s_one, r_one.at[t])

            @pl.when(lax.rem(t, 2) == 1)
            def _():
                along_z(out_g, t, relay_g, t, g, z, x, s_one, r_one.at[t])

        pl.when(t == 0)(plan_x)

        @pl.when(t < N_X)
        def _():
            wait_bytes(wide_x.at[t, pl.ds(0, SIDE - 1)], r_wide.at[t])
            to_peers(t, wide_x[t].reshape(held, width), pick_x)

        pl.when(t == 0)(plan_z)

        @pl.when(t < N_Z)
        def _():
            wait_bytes(wide_z.at[t, pl.ds(0, SIDE - 1)], r_wide.at[N_X + t])
            to_peers(N_X + t, wide_z[t].reshape(held, width), pick_z)

        @pl.when(t == 0)
        def _():
            fill_swap(swap, local, groups)

        @pl.when((t >= 1) & (t < N_G + 1))
        def _():
            c = t - 1
            wait_bytes(relay_g.at[c, pl.ds(0, SIDE - 1)], r_one.at[c])

            @pl.when(lax.rem(c, 2) == 0)
            def _():
                along_z(relay_g, c, rows, 3 * c, g, z, x, s_two, r_rows.at[3 * c])

            @pl.when(lax.rem(c, 2) == 1)
            def _():
                along_x(relay_g, c, rows, 3 * c, g, z, x, s_two, r_rows.at[3 * c])

        @pl.when((t >= 1) & (t < N_X + 1))
        def _():
            c = t - 1
            reorder(c)
            for step in (2, 1, 3):
                peer = ring(z, step)
                remote(
                    y_out.at[c, pl.ds(SIDE * peer, SIDE)], rows.at[3 * c + 1, z], s_end, r_rows.at[3 * c + 1],
                    g, peer, x,
                )
            rows[3 * c + 1, z] = y_out[c, pl.ds(SIDE * z, SIDE)]

        @pl.when((t >= 1) & (t < N_Z + 1))
        def _():
            c = t - 1
            reorder(N_X + c)
            for step in (2, 1, 3):
                peer = ring(x, step)
                remote(
                    y_out.at[N_X + c, pl.ds(SIDE * peer, SIDE)], rows.at[3 * c + 2, :, x], s_end,
                    r_rows.at[3 * c + 2], g, z, peer,
                )
            for p in range(SIDE):
                rows[3 * c + 2, p, x] = y_out[N_X + c, SIDE * x + p]

        @pl.when(t == 1)
        def _():
            def keep(mix):
                put = pltpu.make_async_copy(stage, mix, mix_sem)
                put.start()
                put.wait()

            fill_mix(stage, table[0, 0:local, :], table[0, local : 2 * local, :], float(slots), float(groups), float(seats))
            keep(mix_g)
            fill_mix(stage, table[1, 0 : 2 * local, :], table[1, 2 * local : 4 * local, :], float(SIDE * MOST), float(SIDE), float(tok))
            keep(mix_x)
            fill_mix(stage, table[2, 0 : 2 * local, :], table[2, 2 * local : 4 * local, :], float(SIDE * MOST), float(SIDE), float(tok))
            keep(mix_z)
            seat_t = jnp.transpose(jnp.concatenate([seat, jnp.full((tok - groups, tok), -1.0, F32)], axis=0))
            lane_at = iota((tok, held), 1)
            back = jnp.zeros((tok, held), F32)
            for gg in range(groups):
                column = seat_t[:, gg : gg + 1]
                want = jnp.where(column >= 0, column + float(gg * seats), -1.0)
                back = back + jnp.where(lane_at == want, 1.0, 0.0)
            back_ref[...] = back.astype(BF16)

        def multiply(c, carry_in):
            slot = lax.rem(c, 2)
            wait_bytes(rows.at[c, pl.ds(0, SIDE - 1)], r_rows.at[c])
            for cp in weights(c):
                cp.wait()

            def piece(p, inner):
                at = pl.ds(pl.multiple_of(p * block, block), block)
                part = rows[c, p].reshape(block, width)
                acc_g[at, :] += dot(part, wbuf_g[slot])
                acc_u[at, :] += dot(part, wbuf_u[slot])
                return inner

            lax.fori_loop(0, SIDE, piece, 0)

            @pl.when(c + 2 < CHUNKS)
            def _():
                for cp in weights(c + 2):
                    cp.start()

            return carry_in

        @pl.when(t >= 2)
        def _():
            low = 3 * (t - 2)
            lax.fori_loop(low, jnp.minimum(low + 3, CHUNKS), multiply, 0)

        return carry

    lax.fori_loop(0, N_G + 2, step, 0)

    def finish(b, carry):
        at = pl.ds(pl.multiple_of(b * slots, slots), slots)
        v = acc_g[at, :]
        hid_ref[at, :] = (v / (1.0 + jnp.exp(-v)) * acc_u[at, :]).astype(BF16)
        return carry

    lax.fori_loop(0, total // slots, finish, 0)
    wait_bytes(info_x.at[pl.ds(0, SIDE - 1)], s_info.at[0])
    wait_bytes(info_z.at[pl.ds(0, SIDE - 1)], s_info.at[1])
    wait_bytes(meta_out.at[0, pl.ds(0, groups - 1)], s_meta)
    wait_bytes(first_out.at[:, pl.ds(0, groups - 1)], s_first)
    wait_bytes(wide_x.at[:, pl.ds(0, SIDE - 1)], s_wide_x)
    wait_bytes(wide_z.at[:, pl.ds(0, SIDE - 1)], s_wide_z)
    wait_bytes(out_g.at[:, pl.ds(0, SIDE - 1)], s_one)
    wait_bytes(relay_g.at[:, pl.ds(0, SIDE - 1)], s_two)
    wait_bytes(y_out.at[:, pl.ds(0, SIDE * (SIDE - 1))], s_end)


def return_kernel(
    groups, slots,
    hid_ref, mix_hbm_g, mix_hbm_x, mix_hbm_z, back_ref, wd_ref,
    out_ref,
    out_buf, relay_g, rows_g, mid, y_out, y_in, part_out, part_in, sum_out, sum_in, wbuf, swap, mix_g, mix_x, mix_z,
    s_one, r_one, s_two, r_two, s_mid, r_mid, s_y, r_y, s_last, r_last, s_sum_x, s_sum_z, r_sum, w_sem, mix_sem,
):
    g, z, x = position()
    tok = out_ref.shape[0]
    width = out_ref.shape[1] // CHUNKS
    held = mix_g.shape[0]
    seats = held // groups
    block = SIDE * slots
    total = SIDE * block

    def columns(c):
        return pl.ds(pl.multiple_of(c * width, width), width)

    def weights(c):
        slot = lax.rem(c, 2)
        return pltpu.make_async_copy(wd_ref.at[:, columns(c)], wbuf.at[slot], w_sem.at[slot])

    for c in range(2):
        weights(c).start()
    entry_barrier(g, z, x, groups)
    mixes = [
        pltpu.make_async_copy(mix_hbm_g, mix_g, mix_sem.at[0]),
        pltpu.make_async_copy(mix_hbm_x, mix_x, mix_sem.at[1]),
        pltpu.make_async_copy(mix_hbm_z, mix_z, mix_sem.at[2]),
    ]

    def down(c):
        slot = lax.rem(c, 2)
        weights(c).wait()

        def piece(p, inner):
            at = pl.ds(pl.multiple_of(p * block, block), block)
            got = dot(hid_ref[at, :], wbuf[slot]).astype(BF16)
            out_buf[c, p] = got.reshape(SIDE, slots, width)
            return inner

        lax.fori_loop(0, SIDE, piece, 0)

        @pl.when(c + 2 < CHUNKS)
        def _():
            weights(c + 2).start()

    def to_sources(c):
        wait_bytes(mid.at[c, pl.ds(0, SIDE * (SIDE - 1))], r_mid.at[c])
        src = mid[c].reshape(total, width)
        for p in range(SIDE):
            got = dot(swap[p * block : (p + 1) * block, :], src).astype(BF16)
            y_out[c, pl.ds(p * SIDE, SIDE)] = got.reshape(SIDE, slots, width)
        send_pairs(y_out, y_in, c, g, z, x, groups, s_y, r_y.at[c])

    def weigh(c, mix):
        wait_bytes(y_in.at[c, pl.ds(0, 2 * groups - 2)], r_y.at[c])
        got = dot(mix[...], y_in[c].reshape(total, width)).astype(BF16)
        sum_out[c] = got.reshape(SIDE, tok, width)

    def add_up(c):
        wait_bytes(sum_in.at[c, pl.ds(0, SIDE - 1)], r_sum.at[c])
        got = sum_in[c, 0].astype(F32)
        for b in range(1, SIDE):
            got = got + sum_in[c, b].astype(F32)
        return got.astype(BF16)

    def step(t, carry):
        @pl.when(t < N_G)
        def _():
            down(3 * t)

            @pl.when(lax.rem(t, 2) == 0)
            def _():
                along_x(out_buf, 3 * t, relay_g, t, g, z, x, s_one, r_one.at[t])

            @pl.when(lax.rem(t, 2) == 1)
            def _():
                along_z(out_buf, 3 * t, relay_g, t, g, z, x, s_one, r_one.at[t])

        @pl.when(t < N_X)
        def _():
            c = 3 * t + 1
            down(c)
            for step in (2, 1, 3):
                peer = ring(z, step)
                remote(out_buf.at[c, peer], mid.at[t, pl.ds(SIDE * z, SIDE)], s_mid.at[0], r_mid.at[t], g, peer, x)
            mid[t, pl.ds(SIDE * z, SIDE)] = out_buf[c, z]

        @pl.when(t < N_Z)
        def _():
            c = 3 * t + 2
            down(c)
            for step in (2, 1, 3):
                peer = ring(x, step)
                remote(
                    out_buf.at[c, :, peer], mid.at[N_X + t, pl.ds(SIDE * x, SIDE)], s_mid.at[1],
                    r_mid.at[N_X + t], g, z, peer,
                )
            for p in range(SIDE):
                mid[N_X + t, SIDE * x + p] = out_buf[c, p, x]

        @pl.when(t == 0)
        def _():
            for cp in mixes:
                cp.start()
            fill_swap(swap, groups, SIDE * SIDE)
            for cp in mixes:
                cp.wait()

        @pl.when((t >= 1) & (t < N_G + 1))
        def _():
            c = t - 1
            wait_bytes(relay_g.at[c, pl.ds(0, SIDE - 1)], r_one.at[c])

            @pl.when(lax.rem(c, 2) == 0)
            def _():
                along_z(relay_g, c, rows_g, c, g, z, x, s_two, r_two.at[c])

            @pl.when(lax.rem(c, 2) == 1)
            def _():
                along_x(relay_g, c, rows_g, c, g, z, x, s_two, r_two.at[c])

        @pl.when((t >= 1) & (t < N_X + 1))
        def _():
            to_sources(t - 1)

        @pl.when((t >= 1) & (t < N_Z + 1))
        def _():
            to_sources(N_X + t - 1)

        @pl.when((t >= 2) & (t < N_G + 2))
        def _():
            c = t - 2
            wait_bytes(rows_g.at[c, pl.ds(0, SIDE - 1)], r_two.at[c])
            got = dot(mix_g[...], rows_g[c].reshape(total, width)).astype(BF16)
            part_out[c] = got.reshape(groups, seats, width)
            send_groups(part_out, part_in, c, g, z, x, groups, s_last, r_last.at[c])

        @pl.when((t >= 2) & (t < N_X + 2))
        def _():
            c = t - 2
            weigh(c, mix_x)
            for step in (2, 1, 3):
                peer = ring(x, step)
                remote(sum_out.at[c, peer], sum_in.at[c, x], s_sum_x, r_sum.at[c], g, z, peer)
            sum_in[c, x] = sum_out[c, x]

        @pl.when((t >= 2) & (t < N_Z + 2))
        def _():
            c = N_X + t - 2
            weigh(c, mix_z)
            for step in (2, 1, 3):
                peer = ring(z, step)
                remote(sum_out.at[c, peer], sum_in.at[c, z], s_sum_z, r_sum.at[c], g, peer, x)
            sum_in[c, z] = sum_out[c, z]

        @pl.when((t >= 3) & (t < N_G + 3))
        def _():
            c = t - 3
            wait_bytes(part_in.at[c, pl.ds(0, groups - 1)], r_last.at[c])
            out_ref[:, columns(3 * c)] = dot(back_ref[...], part_in[c].reshape(held, width)).astype(BF16)

        @pl.when((t >= 3) & (t < N_X + 3))
        def _():
            out_ref[:, columns(3 * (t - 3) + 1)] = add_up(t - 3)

        @pl.when((t >= 3) & (t < N_Z + 3))
        def _():
            out_ref[:, columns(3 * (t - 3) + 2)] = add_up(N_X + t - 3)

        return carry

    lax.fori_loop(0, N_G + 3, step, 0)
    wait_bytes(relay_g.at[:, pl.ds(0, SIDE - 1)], s_one)
    wait_bytes(rows_g.at[:, pl.ds(0, SIDE - 1)], s_two)
    wait_bytes(mid.at[pl.ds(0, N_X), pl.ds(0, SIDE * (SIDE - 1))], s_mid.at[0])
    wait_bytes(mid.at[pl.ds(N_X, N_Z), pl.ds(0, SIDE * (SIDE - 1))], s_mid.at[1])
    wait_bytes(y_out.at[:, pl.ds(0, 2 * groups - 2)], s_y)
    wait_bytes(part_out.at[:, pl.ds(0, groups - 1)], s_last)
    wait_bytes(sum_out.at[pl.ds(0, N_X), pl.ds(0, SIDE - 1)], s_sum_x)
    wait_bytes(sum_out.at[pl.ds(N_X, N_Z), pl.ds(0, SIDE - 1)], s_sum_z)


def shards(hidden_states, affinity, group_ids, expert_ids, w_gate, w_up, w_down):
    tok, model = hidden_states.shape
    hid = w_gate.shape[2]
    groups = lax.axis_size("group")
    slots = MOST * groups
    seats = tok * TOPG // groups
    held = groups * seats
    total = SIDE * SIDE * slots
    width = model // CHUNKS
    wide = N_X + N_Z

    vmem = pl.BlockSpec(memory_space=pltpu.VMEM)
    anywhere = pl.BlockSpec(memory_space=pl.ANY)
    dma = pltpu.SemaphoreType.DMA

    def grid4(n):
        return pltpu.VMEM((n, SIDE, SIDE, slots, width), BF16)

    def pairs(n):
        return pltpu.VMEM((n, SIDE * SIDE, slots, width), BF16)

    def seated(n, w):
        return pltpu.VMEM((n, groups, seats, w), BF16)

    def spread(n):
        return pltpu.VMEM((n, SIDE, tok, width), BF16)

    mix_shape = jax.ShapeDtypeStruct((held, total), BF16)
    hidden, mix_g, mix_x, mix_z, back = pl.pallas_call(
        functools.partial(dispatch_kernel, groups, slots),
        out_shape=(
            jax.ShapeDtypeStruct((total, hid), BF16), mix_shape, mix_shape, mix_shape,
            jax.ShapeDtypeStruct((tok, held), BF16),
        ),
        in_specs=[vmem, vmem, vmem, vmem, anywhere, anywhere],
        out_specs=(vmem, anywhere, anywhere, anywhere, vmem),
        scratch_shapes=[
            pltpu.VMEM((tok, LANES), BF16),
            pltpu.VMEM((SIDE, tok, LANES), BF16),
            pltpu.VMEM((SIDE, tok, LANES), BF16),
            seated(1, LANES), seated(1, LANES),
            seated(N_G, width), seated(N_G, width),
            spread(N_X), spread(N_Z),
            grid4(N_G), grid4(N_G),
            pairs(wide), pairs(wide),
            grid4(CHUNKS),
            pltpu.VMEM((total, hid), F32),
            pltpu.VMEM((total, hid), F32),
            pltpu.VMEM((2, width, hid), BF16),
            pltpu.VMEM((2, width, hid), BF16),
            pltpu.VMEM((total, held), BF16),
            pltpu.VMEM((total, held), BF16),
            pltpu.VMEM((total, held), BF16),
            pltpu.VMEM((total, total), BF16),
            pltpu.VMEM((held, tok), BF16),
            pltpu.VMEM((held, total), BF16),
            pltpu.VMEM((3, LANES, held), F32),
            dma((2,)), dma((2,)), dma, dma, dma, dma((N_G,)), dma, dma, dma((wide,)), dma, dma((N_G,)),
            dma, dma((wide,)), dma((wide,)), dma, dma((CHUNKS,)), dma((2, 2)), dma,
        ],
        compiler_params=pltpu.CompilerParams(
            collective_id=0, has_side_effects=True, vmem_limit_bytes=63 * 2**20
        ),
        name="dispatch",
    )(affinity.T, group_ids.T, expert_ids.T, hidden_states, w_gate[0], w_up[0])

    return pl.pallas_call(
        functools.partial(return_kernel, groups, slots),
        out_shape=jax.ShapeDtypeStruct((tok, model), BF16),
        in_specs=[vmem, anywhere, anywhere, anywhere, vmem, anywhere],
        out_specs=vmem,
        scratch_shapes=[
            grid4(CHUNKS), grid4(N_G), grid4(N_G),
            pairs(wide), pairs(wide), pairs(wide),
            seated(N_G, width), seated(N_G, width),
            spread(wide), spread(wide),
            pltpu.VMEM((2, hid, width), BF16),
            pltpu.VMEM((total, total), BF16),
            pltpu.VMEM((held, total), BF16),
            pltpu.VMEM((held, total), BF16),
            pltpu.VMEM((held, total), BF16),
            dma, dma((N_G,)), dma, dma((N_G,)), dma((2,)), dma((wide,)), dma, dma((wide,)),
            dma, dma((N_G,)), dma, dma, dma((wide,)), dma((2,)), dma((3,)),
        ],
        compiler_params=pltpu.CompilerParams(
            collective_id=1, has_side_effects=True, vmem_limit_bytes=60 * 2**20
        ),
        name="giveback",
    )(hidden, mix_g, mix_x, mix_z, back, w_down[0])


def solution(mesh):
    placed = (
        P(("group", "local"), None),
        P(("group", "local"), None),
        P(("group", "local"), None),
        P(("group", "local"), None),
        P(("group", "local"), None, None),
        P(("group", "local"), None, None),
        P(("group", "local"), None, None),
    )
    return jax.shard_map(
        shards, mesh=mesh, in_specs=placed, out_specs=P(("group", "local"), None), check_vma=False
    )
```

```python
import functools

import jax
import jax.numpy as jnp
from jax import lax
from jax.experimental import pallas as pl
from jax.experimental.pallas import tpu as pltpu
from jax.sharding import PartitionSpec as P

TOP_K = 8
TOPG = 4
SIDE = 4
MOST = 10
CHUNKS = 14
N_G = 6
N_X = 4
N_Z = 4
LANES = 128
MESH = pl.DeviceIdType.MESH
BF16 = jnp.bfloat16
F32 = jnp.float32


def position():
    g = lax.axis_index("group")
    l = lax.axis_index("local")
    return g, l // SIDE, l % SIDE


def wait_bytes(ref, sem):
    pltpu.make_async_copy(ref, ref, sem).wait()


def ring(p, step):
    return lax.rem(p + step, SIDE)


def remote(src, dst, ssem, rsem, g, z, x):
    pltpu.make_async_remote_copy(
        src_ref=src, dst_ref=dst, send_sem=ssem, recv_sem=rsem, device_id=(g, z * SIDE + x), device_id_type=MESH
    ).start()


def iota(shape, axis):
    return lax.broadcasted_iota(jnp.int32, shape, axis).astype(F32)


def one_hot(mask):
    return jnp.where(mask, 1.0, 0.0).astype(BF16)


def dot(a, b):
    return jnp.dot(a, b, preferred_element_type=F32)


def signal_peers(sem, g, z, x, groups):
    for step in range(1, groups):
        pl.semaphore_signal(
            sem, inc=1, device_id=(lax.rem(g + step, groups), z * SIDE + x), device_id_type=MESH
        )
    for step in range(1, SIDE):
        pl.semaphore_signal(sem, inc=1, device_id=(g, ring(z, step) * SIDE + x), device_id_type=MESH)
        pl.semaphore_signal(sem, inc=1, device_id=(g, z * SIDE + ring(x, step)), device_id_type=MESH)


def entry_barrier(g, z, x, groups):
    bar = pltpu.get_barrier_semaphore()
    signal_peers(bar, g, z, x, groups)
    pl.semaphore_wait(bar, groups - 1 + 2 * (SIDE - 1))


def send_groups(src, dst, c, g, z, x, groups, ssem, rsem):
    for step in range(1, groups):
        peer = lax.rem(g + step, groups)
        remote(src.at[c, peer], dst.at[c, g], ssem, rsem, peer, z, x)
    dst[c, g] = src[c, g]


def send_pairs(src, dst, c, g, z, x, groups, ssem, rsem):
    for step in range(1, groups):
        peer = lax.rem(g + step, groups)
        remote(src.at[c, pl.ds(2 * peer, 2)], dst.at[c, pl.ds(2 * g, 2)], ssem, rsem, peer, z, x)
    dst[c, pl.ds(2 * g, 2)] = src[c, pl.ds(2 * g, 2)]


def along_z(src, sc, dst, dc, g, z, x, ssem, rsem):
    for step in (2, 1, 3):
        peer = ring(z, step)
        remote(src.at[sc, peer], dst.at[dc, z], ssem, rsem, g, peer, x)
    dst[dc, z] = src[sc, z]


def along_x(src, sc, dst, dc, g, z, x, ssem, rsem):
    for step in (2, 1, 3):
        peer = ring(x, step)
        remote(src.at[sc, :, peer], dst.at[dc, :, x], ssem, rsem, g, z, peer)
    for row in range(SIDE):
        dst[dc, row, x] = src[sc, row, x]


def rank_table(eids, mixes, experts, span):
    rows, cols = experts.shape
    named = jnp.zeros((rows, cols), F32)
    weight = jnp.zeros((rows, cols), F32)
    for k in range(TOP_K):
        hit = eids[k] == experts
        named = named + jnp.where(hit, 1.0, 0.0)
        weight = weight + jnp.where(hit, mixes[k], 0.0)
    r = iota((cols, cols), 0)
    c = iota((cols, cols), 1)
    earlier = one_hot((r < c) & (jnp.floor(r / span) == jnp.floor(c / span)))
    ahead = dot(named.astype(BF16), earlier)
    return jnp.where(named > 0, ahead, -1.0), weight


def fill_pick(pick, seat, per_expert, blocks, span):
    total, cols = pick.shape
    rows = seat.shape[0]
    part = total // SIDE
    seat16 = seat.astype(BF16)
    column = 16.0 * jnp.floor(iota((part, cols), 1) / span)
    for p in range(SIDE):
        at = iota((part, rows), 0) + float(p * part)
        spread = one_hot(jnp.floor((at + 0.5) / per_expert) == iota((part, rows), 1))
        slot = iota((part, 1), 0) + float(p * part)
        ten = jnp.floor((slot + 0.5) / MOST)
        code = (slot - MOST * ten) + 16.0 * (ten - blocks * jnp.floor((ten + 0.5) / blocks))
        pick[p * part : (p + 1) * part, :] = one_hot(dot(spread, seat16) + column == code)


def fill_mix(mix, seat, weight, per_expert, blocks, span):
    cols, total = mix.shape
    rows = seat.shape[0]
    both = jnp.concatenate([seat, weight, jnp.zeros((LANES - 2 * rows, cols), F32)], axis=0)
    turned = jnp.transpose(both).astype(BF16)
    owner = jnp.floor((iota((LANES, total), 1) + 0.5) / per_expert)
    lane = iota((LANES, total), 0)
    spread_seat = one_hot(owner == lane)
    spread_mix = one_hot(owner + float(rows) == lane)
    slot = iota((1, total), 1)
    ten = jnp.floor((slot + 0.5) / MOST)
    code = (slot - MOST * ten) + 16.0 * (ten - blocks * jnp.floor((ten + 0.5) / blocks))
    part = cols // SIDE
    for p in range(SIDE):
        here = turned[p * part : (p + 1) * part, :]
        row = 16.0 * jnp.floor((iota((part, 1), 0) + float(p * part)) / span)
        mix[p * part : (p + 1) * part, :] = jnp.where(
            dot(here, spread_seat) + row == code, dot(here, spread_mix), 0.0
        ).astype(BF16)


def fill_swap(swap, outer, inner):
    total = swap.shape[0]
    part = total // SIDE
    lane = iota((part, total), 1)
    for p in range(SIDE):
        slot = iota((part, 1), 0) + float(p * part)
        ten = jnp.floor((slot + 0.5) / MOST)
        o = jnp.floor((ten + 0.5) / inner)
        i = ten - o * inner
        swap[p * part : (p + 1) * part, :] = one_hot(lane == (i * outer + o) * MOST + (slot - MOST * ten))


def read_info(info):
    ids = []
    mixes = []
    for k in range(TOP_K):
        inside = info[k : k + 1, :]
        group = info[2 * TOP_K + k // 2 : 2 * TOP_K + k // 2 + 1, :]
        ids.append(jnp.where(inside >= 0, inside + float(SIDE * SIDE) * group, -1.0))
        mixes.append(info[TOP_K + k : TOP_K + k + 1, :])
    return ids, mixes


def dispatch_kernel(
    groups, slots,
    aff_ref, gid_ref, eid_ref, tok_ref, wg_ref, wu_ref,
    hid_ref, mix_g, mix_x, mix_z, back_ref,
    info_out, info_x, info_z, meta_out, meta_in, first_out, first_in, wide_x, wide_z,
    out_g, relay_g, y_out, y_in, rows, acc_g, acc_u, wbuf_g, wbuf_u, pick_g, pick_x, pick_z, swap, sel, stage, table,
    s_info, r_info, s_meta, r_meta, s_first, r_first, s_wide_x, s_wide_z, r_wide, s_one, r_one,
    s_two, s_y, r_y, s_end, r_rows, w_sem, mix_sem,
):
    g, z, x = position()
    tok = tok_ref.shape[0]
    width = tok_ref.shape[1] // CHUNKS
    seats = tok * TOPG // groups
    held = groups * seats
    block = SIDE * slots
    total = SIDE * block
    local = SIDE * SIDE

    def columns(c):
        return pl.ds(pl.multiple_of(c * width, width), width)

    def group_at_step(t):
        return jnp.minimum(2 * t, t + 2)

    def step_column(t):
        return jnp.minimum(4 * t, 3 * t + 2)

    def group_column(k):
        return k // 2 * 4 + k % 2 + 2 * (k // 5)

    def weights(c):
        slot = lax.rem(c, 2)
        return (
            pltpu.make_async_copy(wg_ref.at[columns(c)], wbuf_g.at[slot], w_sem.at[0, slot]),
            pltpu.make_async_copy(wu_ref.at[columns(c)], wbuf_u.at[slot], w_sem.at[1, slot]),
        )

    for c in range(2):
        for cp in weights(c):
            cp.start()

    aff = aff_ref[...]
    scaled = (2.5 * aff / jnp.sum(aff, axis=0, keepdims=True)).astype(BF16).astype(F32)
    gid = gid_ref[...].astype(F32)
    eid = eid_ref[...].astype(F32)
    owner = jnp.floor(eid / float(local))
    chosen = jnp.concatenate([gid[k // 2 : k // 2 + 1, :] for k in range(TOP_K)], axis=0)
    is_valid = owner == chosen
    mixing = jnp.where(is_valid, scaled, 0.0)
    inside = jnp.where(is_valid, eid - float(local) * owner, -1.0)
    rt_t = jnp.concatenate(
        [inside, mixing, gid, jnp.zeros((LANES - 2 * TOP_K - TOPG, tok), F32)], axis=0
    )
    rt = jnp.transpose(rt_t)
    info_out[...] = rt.astype(BF16)
    info_x[x] = info_out[...]
    info_z[z] = info_out[...]

    entry_barrier(g, z, x, groups)
    for step in (2, 1, 3):
        peer = ring(x, step)
        remote(info_out, info_x.at[x], s_info.at[0], r_info.at[0], g, z, peer)
        peer = ring(z, step)
        remote(info_out, info_z.at[z], s_info.at[1], r_info.at[1], g, peer, x)

    group_at = iota((groups, tok), 0)
    member = jnp.zeros((groups, tok), F32)
    for j in range(TOPG):
        member = member + jnp.where(rt_t[2 * TOP_K + j : 2 * TOP_K + j + 1, :] == group_at, 1.0, 0.0)
    earlier = one_hot(iota((tok, tok), 0) < iota((tok, tok), 1))
    seat = jnp.where(member > 0, dot(member.astype(BF16), earlier), -1.0)
    seat_at = iota((seats, tok), 0)
    for gg in range(groups):
        sel[gg * seats : (gg + 1) * seats, :] = one_hot(seat_at == seat[gg : gg + 1, :])
    meta_out[0] = dot(sel[...], info_out[...]).astype(BF16).reshape(groups, seats, LANES)
    send_groups(meta_out, meta_in, 0, g, z, x, groups, s_meta, r_meta)

    def first(t, carry):
        got = dot(sel[...], tok_ref[:, columns(group_column(t))]).astype(BF16)
        first_out[t] = got.reshape(groups, seats, width)
        send_groups(first_out, first_in, t, g, z, x, groups, s_first, r_first.at[t])

        @pl.when(t < N_X)
        def _():
            wide_x[t, x] = tok_ref[:, columns(step_column(t + 1) - 2)]
            for step in (2, 1, 3):
                remote(wide_x.at[t, x], wide_x.at[t, x], s_wide_x, r_wide.at[t], g, z, ring(x, step))
            wide_z[t, z] = tok_ref[:, columns(step_column(t + 1) - 1)]
            for step in (2, 1, 3):
                remote(wide_z.at[t, z], wide_z.at[t, z], s_wide_z, r_wide.at[N_X + t], g, ring(z, step), x)

        return carry

    lax.fori_loop(0, N_G, first, 0)

    def clear(b, carry):
        at = pl.ds(pl.multiple_of(b * slots, slots), slots)
        acc_g[at, :] = jnp.zeros((slots, acc_g.shape[1]), F32)
        acc_u[at, :] = jnp.zeros((slots, acc_u.shape[1]), F32)
        return carry

    lax.fori_loop(0, total // slots, clear, 0)

    def plan_g():
        wait_bytes(meta_in.at[0, pl.ds(0, groups - 1)], r_meta)
        ids, mixes = read_info(jnp.transpose(meta_in[0].reshape(held, LANES).astype(F32)))
        own = iota((local, held), 0) + float(local) * g.astype(F32)
        seat_in, weight = rank_table(ids, mixes, own, float(seats))
        fill_pick(pick_g, seat_in, float(slots), float(groups), float(seats))
        table[0, 0:local, :] = seat_in
        table[0, local : 2 * local, :] = weight

    def plan_wide(info, which, own, pick):
        wait_bytes(info.at[pl.ds(0, SIDE - 1)], r_info.at[which])
        ids, mixes = read_info(jnp.transpose(info[...].reshape(held, LANES).astype(F32)))
        seat_in, weight = rank_table(ids, mixes, own, float(tok))
        fill_pick(pick, seat_in, float(SIDE * MOST), float(SIDE), float(tok))
        table[1 + which, 0 : 2 * local, :] = seat_in
        table[1 + which, 2 * local : 4 * local, :] = weight

    def plan_x():
        plan_wide(info_x, 0, iota((2 * local, held), 0) * float(SIDE) + x.astype(F32), pick_x)

    def plan_z():
        row = iota((2 * local, held), 0)
        own = jnp.floor(row / float(SIDE)) * float(local - SIDE) + row + float(SIDE) * z.astype(F32)
        plan_wide(info_z, 1, own, pick_z)

    plan_g()

    def to_peers(c, src, pick):
        for p in range(SIDE):
            got = dot(pick[p * block : (p + 1) * block, :], src).astype(BF16)
            y_out[c, pl.ds(p * SIDE, SIDE)] = got.reshape(SIDE, slots, width)
        send_pairs(y_out, y_in, c, g, z, x, groups, s_y.at[c], r_y.at[c])

    def reorder(c):
        wait_bytes(y_in.at[c, pl.ds(0, 2 * groups - 2)], r_y.at[c])
        wait_bytes(y_out.at[c, pl.ds(0, 2 * groups - 2)], s_y.at[c])
        src = y_in[c].reshape(total, width)
        for p in range(SIDE):
            got = dot(swap[p * block : (p + 1) * block, :], src).astype(BF16)
            y_out[c, pl.ds(p * SIDE, SIDE)] = got.reshape(SIDE, slots, width)

    def step(t, carry):
        def spread_group(k, inner):
            wait_bytes(first_in.at[k, pl.ds(0, groups - 1)], r_first.at[k])
            src = first_in[k].reshape(held, width)
            for p in range(SIDE):
                got = dot(pick_g[p * block : (p + 1) * block, :], src).astype(BF16)
                out_g[k, p] = got.reshape(SIDE, slots, width)

            @pl.when(lax.rem(k, 2) == 0)
            def _():
                along_x(out_g, k, relay_g, k, g, z, x, s_one, r_one.at[k])

            @pl.when(lax.rem(k, 2) == 1)
            def _():
                along_z(out_g, k, relay_g, k, g, z, x, s_one, r_one.at[k])

            return inner

        @pl.when(t < N_X)
        def _():
            lax.fori_loop(group_at_step(t), group_at_step(t + 1), spread_group, 0)

        pl.when(t == 0)(plan_x)

        @pl.when(t < N_X)
        def _():
            wait_bytes(wide_x.at[t, pl.ds(0, SIDE - 1)], r_wide.at[t])
            to_peers(t, wide_x[t].reshape(held, width), pick_x)

        pl.when(t == 0)(plan_z)

        @pl.when(t < N_Z)
        def _():
            wait_bytes(wide_z.at[t, pl.ds(0, SIDE - 1)], r_wide.at[N_X + t])
            to_peers(N_X + t, wide_z[t].reshape(held, width), pick_z)

        @pl.when(t == 0)
        def _():
            fill_swap(swap, local, groups)

        def pass_group(k, inner):
            wait_bytes(relay_g.at[k, pl.ds(0, SIDE - 1)], r_one.at[k])

            @pl.when(lax.rem(k, 2) == 0)
            def _():
                along_z(relay_g, k, rows, group_column(k), g, z, x, s_two, r_rows.at[group_column(k)])

            @pl.when(lax.rem(k, 2) == 1)
            def _():
                along_x(relay_g, k, rows, group_column(k), g, z, x, s_two, r_rows.at[group_column(k)])

            return inner

        @pl.when((t >= 1) & (t < N_X + 1))
        def _():
            lax.fori_loop(group_at_step(t - 1), group_at_step(t), pass_group, 0)

        @pl.when((t >= 1) & (t < N_X + 1))
        def _():
            c = t - 1
            reorder(c)
            for step in (2, 1, 3):
                peer = ring(z, step)
                remote(
                    y_out.at[c, pl.ds(SIDE * peer, SIDE)], rows.at[step_column(t) - 2, z], s_end, r_rows.at[step_column(t) - 2],
                    g, peer, x,
                )
            rows[step_column(t) - 2, z] = y_out[c, pl.ds(SIDE * z, SIDE)]

        @pl.when((t >= 1) & (t < N_Z + 1))
        def _():
            c = t - 1
            reorder(N_X + c)
            for step in (2, 1, 3):
                peer = ring(x, step)
                remote(
                    y_out.at[N_X + c, pl.ds(SIDE * peer, SIDE)], rows.at[step_column(t) - 1, :, x], s_end,
                    r_rows.at[step_column(t) - 1], g, z, peer,
                )
            for p in range(SIDE):
                rows[step_column(t) - 1, p, x] = y_out[N_X + c, SIDE * x + p]

        @pl.when(t == 1)
        def _():
            def keep(mix):
                put = pltpu.make_async_copy(stage, mix, mix_sem)
                put.start()
                put.wait()

            fill_mix(stage, table[0, 0:local, :], table[0, local : 2 * local, :], float(slots), float(groups), float(seats))
            keep(mix_g)
            fill_mix(stage, table[1, 0 : 2 * local, :], table[1, 2 * local : 4 * local, :], float(SIDE * MOST), float(SIDE), float(tok))
            keep(mix_x)
            fill_mix(stage, table[2, 0 : 2 * local, :], table[2, 2 * local : 4 * local, :], float(SIDE * MOST), float(SIDE), float(tok))
            keep(mix_z)
            seat_t = jnp.transpose(jnp.concatenate([seat, jnp.full((tok - groups, tok), -1.0, F32)], axis=0))
            lane_at = iota((tok, held), 1)
            back = jnp.zeros((tok, held), F32)
            for gg in range(groups):
                column = seat_t[:, gg : gg + 1]
                want = jnp.where(column >= 0, column + float(gg * seats), -1.0)
                back = back + jnp.where(lane_at == want, 1.0, 0.0)
            back_ref[...] = back.astype(BF16)

        def multiply(c, carry_in):
            slot = lax.rem(c, 2)
            wait_bytes(rows.at[c, pl.ds(0, SIDE - 1)], r_rows.at[c])
            for cp in weights(c):
                cp.wait()

            def piece(p, inner):
                at = pl.ds(pl.multiple_of(p * block, block), block)
                part = rows[c, p].reshape(block, width)
                acc_g[at, :] += dot(part, wbuf_g[slot])
                acc_u[at, :] += dot(part, wbuf_u[slot])
                return inner

            lax.fori_loop(0, SIDE, piece, 0)

            @pl.when(c + 2 < CHUNKS)
            def _():
                for cp in weights(c + 2):
                    cp.start()

            return carry_in

        @pl.when(t >= 2)
        def _():
            c = t - 2
            lax.fori_loop(step_column(c), step_column(c + 1), multiply, 0)

        return carry

    lax.fori_loop(0, N_X + 2, step, 0)

    def finish(b, carry):
        at = pl.ds(pl.multiple_of(b * slots, slots), slots)
        v = acc_g[at, :]
        hid_ref[at, :] = (v / (1.0 + jnp.exp(-v)) * acc_u[at, :]).astype(BF16)
        return carry

    lax.fori_loop(0, total // slots, finish, 0)
    wait_bytes(info_x.at[pl.ds(0, SIDE - 1)], s_info.at[0])
    wait_bytes(info_z.at[pl.ds(0, SIDE - 1)], s_info.at[1])
    wait_bytes(meta_out.at[0, pl.ds(0, groups - 1)], s_meta)
    wait_bytes(first_out.at[:, pl.ds(0, groups - 1)], s_first)
    wait_bytes(wide_x.at[:, pl.ds(0, SIDE - 1)], s_wide_x)
    wait_bytes(wide_z.at[:, pl.ds(0, SIDE - 1)], s_wide_z)
    wait_bytes(out_g.at[:, pl.ds(0, SIDE - 1)], s_one)
    wait_bytes(relay_g.at[:, pl.ds(0, SIDE - 1)], s_two)
    wait_bytes(y_out.at[:, pl.ds(0, SIDE * (SIDE - 1))], s_end)


def return_kernel(
    groups, slots,
    hid_ref, mix_hbm_g, mix_hbm_x, mix_hbm_z, back_ref, wd_ref,
    out_ref,
    out_buf, relay_g, rows_g, mid, y_out, y_in, part_out, part_in, sum_out, sum_in, wbuf, swap, mix_g, mix_x, mix_z,
    s_one, r_one, s_two, r_two, s_mid, r_mid, s_y, r_y, s_last, r_last, s_sum_x, s_sum_z, r_sum, w_sem, mix_sem,
):
    g, z, x = position()
    tok = out_ref.shape[0]
    width = out_ref.shape[1] // CHUNKS
    held = mix_g.shape[0]
    seats = held // groups
    block = SIDE * slots
    total = SIDE * block

    def columns(c):
        return pl.ds(pl.multiple_of(c * width, width), width)

    def group_at_step(t):
        return jnp.maximum(jnp.minimum(2 * t - 1, t + 2), 0)

    def step_column(t):
        return 2 * t + group_at_step(t)

    def group_column(k):
        return 2 * ((k + 1) // 2) + 2 + k

    def weights(c):
        slot = lax.rem(c, 2)
        return pltpu.make_async_copy(wd_ref.at[:, columns(c)], wbuf.at[slot], w_sem.at[slot])

    for c in range(2):
        weights(c).start()
    entry_barrier(g, z, x, groups)
    mixes = [
        pltpu.make_async_copy(mix_hbm_g, mix_g, mix_sem.at[0]),
        pltpu.make_async_copy(mix_hbm_x, mix_x, mix_sem.at[1]),
        pltpu.make_async_copy(mix_hbm_z, mix_z, mix_sem.at[2]),
    ]

    def down(c):
        slot = lax.rem(c, 2)
        weights(c).wait()

        def piece(p, inner):
            at = pl.ds(pl.multiple_of(p * block, block), block)
            got = dot(hid_ref[at, :], wbuf[slot]).astype(BF16)
            out_buf[c, p] = got.reshape(SIDE, slots, width)
            return inner

        lax.fori_loop(0, SIDE, piece, 0)

        @pl.when(c + 2 < CHUNKS)
        def _():
            weights(c + 2).start()

    def to_sources(c):
        wait_bytes(mid.at[c, pl.ds(0, SIDE * (SIDE - 1))], r_mid.at[c])
        src = mid[c].reshape(total, width)
        for p in range(SIDE):
            got = dot(swap[p * block : (p + 1) * block, :], src).astype(BF16)
            y_out[c, pl.ds(p * SIDE, SIDE)] = got.reshape(SIDE, slots, width)
        send_pairs(y_out, y_in, c, g, z, x, groups, s_y, r_y.at[c])

    def weigh(c, mix):
        wait_bytes(y_in.at[c, pl.ds(0, 2 * groups - 2)], r_y.at[c])
        got = dot(mix[...], y_in[c].reshape(total, width)).astype(BF16)
        sum_out[c] = got.reshape(SIDE, tok, width)

    def add_up(c):
        wait_bytes(sum_in.at[c, pl.ds(0, SIDE - 1)], r_sum.at[c])
        got = sum_in[c, 0].astype(F32)
        for b in range(1, SIDE):
            got = got + sum_in[c, b].astype(F32)
        return got.astype(BF16)

    def step(t, carry):
        @pl.when(t < N_X)
        def _():
            c = step_column(t)
            down(c)
            for step in (2, 1, 3):
                peer = ring(z, step)
                remote(out_buf.at[c, peer], mid.at[t, pl.ds(SIDE * z, SIDE)], s_mid.at[0], r_mid.at[t], g, peer, x)
            mid[t, pl.ds(SIDE * z, SIDE)] = out_buf[c, z]

        @pl.when(t < N_Z)
        def _():
            c = step_column(t) + 1
            down(c)
            for step in (2, 1, 3):
                peer = ring(x, step)
                remote(
                    out_buf.at[c, :, peer], mid.at[N_X + t, pl.ds(SIDE * x, SIDE)], s_mid.at[1],
                    r_mid.at[N_X + t], g, z, peer,
                )
            for p in range(SIDE):
                mid[N_X + t, SIDE * x + p] = out_buf[c, p, x]

        def start_group(k, inner):
            c = group_column(k)
            down(c)

            @pl.when(lax.rem(k, 2) == 0)
            def _():
                along_x(out_buf, c, relay_g, k, g, z, x, s_one, r_one.at[k])

            @pl.when(lax.rem(k, 2) == 1)
            def _():
                along_z(out_buf, c, relay_g, k, g, z, x, s_one, r_one.at[k])

            return inner

        @pl.when(t < N_X)
        def _():
            lax.fori_loop(group_at_step(t), group_at_step(t + 1), start_group, 0)

        @pl.when(t == 0)
        def _():
            for cp in mixes:
                cp.start()
            fill_swap(swap, groups, SIDE * SIDE)
            for cp in mixes:
                cp.wait()

        @pl.when((t >= 1) & (t < N_X + 1))
        def _():
            to_sources(t - 1)

        @pl.when((t >= 1) & (t < N_Z + 1))
        def _():
            to_sources(N_X + t - 1)

        def pass_group(k, inner):
            wait_bytes(relay_g.at[k, pl.ds(0, SIDE - 1)], r_one.at[k])

            @pl.when(lax.rem(k, 2) == 0)
            def _():
                along_z(relay_g, k, rows_g, k, g, z, x, s_two, r_two.at[k])

            @pl.when(lax.rem(k, 2) == 1)
            def _():
                along_x(relay_g, k, rows_g, k, g, z, x, s_two, r_two.at[k])

            return inner

        @pl.when((t >= 1) & (t < N_X + 1))
        def _():
            lax.fori_loop(group_at_step(t - 1), group_at_step(t), pass_group, 0)

        @pl.when((t >= 2) & (t < N_X + 2))
        def _():
            c = t - 2
            weigh(c, mix_x)
            for step in (2, 1, 3):
                peer = ring(x, step)
                remote(sum_out.at[c, peer], sum_in.at[c, x], s_sum_x, r_sum.at[c], g, z, peer)
            sum_in[c, x] = sum_out[c, x]

        @pl.when((t >= 2) & (t < N_Z + 2))
        def _():
            c = N_X + t - 2
            weigh(c, mix_z)
            for step in (2, 1, 3):
                peer = ring(z, step)
                remote(sum_out.at[c, peer], sum_in.at[c, z], s_sum_z, r_sum.at[c], g, peer, x)
            sum_in[c, z] = sum_out[c, z]

        def weigh_group(k, inner):
            wait_bytes(rows_g.at[k, pl.ds(0, SIDE - 1)], r_two.at[k])
            got = dot(mix_g[...], rows_g[k].reshape(total, width)).astype(BF16)
            part_out[k] = got.reshape(groups, seats, width)
            send_groups(part_out, part_in, k, g, z, x, groups, s_last, r_last.at[k])
            return inner

        @pl.when((t >= 2) & (t < N_X + 2))
        def _():
            lax.fori_loop(group_at_step(t - 2), group_at_step(t - 1), weigh_group, 0)

        def place_group(k, inner):
            wait_bytes(part_in.at[k, pl.ds(0, groups - 1)], r_last.at[k])
            out_ref[:, columns(group_column(k))] = dot(back_ref[...], part_in[k].reshape(held, width)).astype(BF16)
            return inner

        @pl.when((t >= 3) & (t < N_X + 3))
        def _():
            lax.fori_loop(group_at_step(t - 3), group_at_step(t - 2), place_group, 0)

        @pl.when((t >= 3) & (t < N_X + 3))
        def _():
            out_ref[:, columns(step_column(t - 3))] = add_up(t - 3)

        @pl.when((t >= 3) & (t < N_Z + 3))
        def _():
            out_ref[:, columns(step_column(t - 3) + 1)] = add_up(N_X + t - 3)

        return carry

    lax.fori_loop(0, N_X + 3, step, 0)
    wait_bytes(relay_g.at[:, pl.ds(0, SIDE - 1)], s_one)
    wait_bytes(rows_g.at[:, pl.ds(0, SIDE - 1)], s_two)
    wait_bytes(mid.at[pl.ds(0, N_X), pl.ds(0, SIDE * (SIDE - 1))], s_mid.at[0])
    wait_bytes(mid.at[pl.ds(N_X, N_Z), pl.ds(0, SIDE * (SIDE - 1))], s_mid.at[1])
    wait_bytes(y_out.at[:, pl.ds(0, 2 * groups - 2)], s_y)
    wait_bytes(part_out.at[:, pl.ds(0, groups - 1)], s_last)
    wait_bytes(sum_out.at[pl.ds(0, N_X), pl.ds(0, SIDE - 1)], s_sum_x)
    wait_bytes(sum_out.at[pl.ds(N_X, N_Z), pl.ds(0, SIDE - 1)], s_sum_z)


def shards(hidden_states, affinity, group_ids, expert_ids, w_gate, w_up, w_down):
    tok, model = hidden_states.shape
    hid = w_gate.shape[2]
    groups = lax.axis_size("group")
    slots = MOST * groups
    seats = tok * TOPG // groups
    held = groups * seats
    total = SIDE * SIDE * slots
    width = model // CHUNKS
    wide = N_X + N_Z

    vmem = pl.BlockSpec(memory_space=pltpu.VMEM)
    anywhere = pl.BlockSpec(memory_space=pl.ANY)
    dma = pltpu.SemaphoreType.DMA

    def grid4(n):
        return pltpu.VMEM((n, SIDE, SIDE, slots, width), BF16)

    def pairs(n):
        return pltpu.VMEM((n, SIDE * SIDE, slots, width), BF16)

    def seated(n, w):
        return pltpu.VMEM((n, groups, seats, w), BF16)

    def spread(n):
        return pltpu.VMEM((n, SIDE, tok, width), BF16)

    mix_shape = jax.ShapeDtypeStruct((held, total), BF16)
    hidden, mix_g, mix_x, mix_z, back = pl.pallas_call(
        functools.partial(dispatch_kernel, groups, slots),
        out_shape=(
            jax.ShapeDtypeStruct((total, hid), BF16), mix_shape, mix_shape, mix_shape,
            jax.ShapeDtypeStruct((tok, held), BF16),
        ),
        in_specs=[vmem, vmem, vmem, vmem, anywhere, anywhere],
        out_specs=(vmem, anywhere, anywhere, anywhere, vmem),
        scratch_shapes=[
            pltpu.VMEM((tok, LANES), BF16),
            pltpu.VMEM((SIDE, tok, LANES), BF16),
            pltpu.VMEM((SIDE, tok, LANES), BF16),
            seated(1, LANES), seated(1, LANES),
            seated(N_G, width), seated(N_G, width),
            spread(N_X), spread(N_Z),
            grid4(N_G), grid4(N_G),
            pairs(wide), pairs(wide),
            grid4(CHUNKS),
            pltpu.VMEM((total, hid), F32),
            pltpu.VMEM((total, hid), F32),
            pltpu.VMEM((2, width, hid), BF16),
            pltpu.VMEM((2, width, hid), BF16),
            pltpu.VMEM((total, held), BF16),
            pltpu.VMEM((total, held), BF16),
            pltpu.VMEM((total, held), BF16),
            pltpu.VMEM((total, total), BF16),
            pltpu.VMEM((held, tok), BF16),
            pltpu.VMEM((held, total), BF16),
            pltpu.VMEM((3, LANES, held), F32),
            dma((2,)), dma((2,)), dma, dma, dma, dma((N_G,)), dma, dma, dma((wide,)), dma, dma((N_G,)),
            dma, dma((wide,)), dma((wide,)), dma, dma((CHUNKS,)), dma((2, 2)), dma,
        ],
        compiler_params=pltpu.CompilerParams(
            collective_id=0, has_side_effects=True, vmem_limit_bytes=63 * 2**20
        ),
        name="dispatch",
    )(affinity.T, group_ids.T, expert_ids.T, hidden_states, w_gate[0], w_up[0])

    return pl.pallas_call(
        functools.partial(return_kernel, groups, slots),
        out_shape=jax.ShapeDtypeStruct((tok, model), BF16),
        in_specs=[vmem, anywhere, anywhere, anywhere, vmem, anywhere],
        out_specs=vmem,
        scratch_shapes=[
            grid4(CHUNKS), grid4(N_G), grid4(N_G),
            pairs(wide), pairs(wide), pairs(wide),
            seated(N_G, width), seated(N_G, width),
            spread(wide), spread(wide),
            pltpu.VMEM((2, hid, width), BF16),
            pltpu.VMEM((total, total), BF16),
            pltpu.VMEM((held, total), BF16),
            pltpu.VMEM((held, total), BF16),
            pltpu.VMEM((held, total), BF16),
            dma, dma((N_G,)), dma, dma((N_G,)), dma((2,)), dma((wide,)), dma, dma((wide,)),
            dma, dma((N_G,)), dma, dma, dma((wide,)), dma((2,)), dma((3,)),
        ],
        compiler_params=pltpu.CompilerParams(
            collective_id=1, has_side_effects=True, vmem_limit_bytes=60 * 2**20
        ),
        name="giveback",
    )(hidden, mix_g, mix_x, mix_z, back, w_down[0])


def solution(mesh):
    placed = (
        P(("group", "local"), None),
        P(("group", "local"), None),
        P(("group", "local"), None),
        P(("group", "local"), None),
        P(("group", "local"), None, None),
        P(("group", "local"), None, None),
        P(("group", "local"), None, None),
    )
    return jax.shard_map(
        shards, mesh=mesh, in_specs=placed, out_specs=P(("group", "local"), None), check_vma=False
    )
```

```python
import functools

import jax
import jax.numpy as jnp
from jax import lax
from jax.experimental import pallas as pl
from jax.experimental.pallas import tpu as pltpu
from jax.sharding import PartitionSpec as P

TOP_K = 8
TOPG = 4
SIDE = 4
MOST = 10
CHUNKS = 14
N_G = 6
N_X = 4
N_Z = 4
LANES = 128
MESH = pl.DeviceIdType.MESH
BF16 = jnp.bfloat16
F32 = jnp.float32


def position():
    g = lax.axis_index("group")
    l = lax.axis_index("local")
    return g, l // SIDE, l % SIDE


def wait_bytes(ref, sem):
    pltpu.make_async_copy(ref, ref, sem).wait()


def ring(p, step):
    return lax.rem(p + step, SIDE)


def remote(src, dst, ssem, rsem, g, z, x):
    pltpu.make_async_remote_copy(
        src_ref=src, dst_ref=dst, send_sem=ssem, recv_sem=rsem, device_id=(g, z * SIDE + x), device_id_type=MESH
    ).start()


def iota(shape, axis):
    return lax.broadcasted_iota(jnp.int32, shape, axis).astype(F32)


def one_hot(mask):
    return jnp.where(mask, 1.0, 0.0).astype(BF16)


def dot(a, b):
    return jnp.dot(a, b, preferred_element_type=F32)


def signal_peers(sem, g, z, x, groups):
    for step in range(1, groups):
        pl.semaphore_signal(
            sem, inc=1, device_id=(lax.rem(g + step, groups), z * SIDE + x), device_id_type=MESH
        )
    for step in range(1, SIDE):
        pl.semaphore_signal(sem, inc=1, device_id=(g, ring(z, step) * SIDE + x), device_id_type=MESH)
        pl.semaphore_signal(sem, inc=1, device_id=(g, z * SIDE + ring(x, step)), device_id_type=MESH)


def barrier_signal(g, z, x, groups):
    signal_peers(pltpu.get_barrier_semaphore(), g, z, x, groups)


def barrier_wait(groups):
    pl.semaphore_wait(pltpu.get_barrier_semaphore(), groups - 1 + 2 * (SIDE - 1))


def send_groups(src, dst, c, g, z, x, groups, ssem, rsem):
    for step in range(1, groups):
        peer = lax.rem(g + step, groups)
        remote(src.at[c, peer], dst.at[c, g], ssem, rsem, peer, z, x)
    dst[c, g] = src[c, g]


def send_pairs(src, dst, c, g, z, x, groups, ssem, rsem):
    for step in range(1, groups):
        peer = lax.rem(g + step, groups)
        remote(src.at[c, pl.ds(2 * peer, 2)], dst.at[c, pl.ds(2 * g, 2)], ssem, rsem, peer, z, x)
    dst[c, pl.ds(2 * g, 2)] = src[c, pl.ds(2 * g, 2)]


def along_z(src, sc, dst, dc, g, z, x, ssem, rsem):
    for step in (2, 1, 3):
        peer = ring(z, step)
        remote(src.at[sc, peer], dst.at[dc, z], ssem, rsem, g, peer, x)
    dst[dc, z] = src[sc, z]


def along_x(src, sc, dst, dc, g, z, x, ssem, rsem):
    for step in (2, 1, 3):
        peer = ring(x, step)
        remote(src.at[sc, :, peer], dst.at[dc, :, x], ssem, rsem, g, z, peer)
    for row in range(SIDE):
        dst[dc, row, x] = src[sc, row, x]


def rank_table(eids, mixes, experts, span):
    rows, cols = experts.shape
    named = jnp.zeros((rows, cols), F32)
    weight = jnp.zeros((rows, cols), F32)
    for k in range(TOP_K):
        hit = eids[k] == experts
        named = named + jnp.where(hit, 1.0, 0.0)
        weight = weight + jnp.where(hit, mixes[k], 0.0)
    r = iota((cols, cols), 0)
    c = iota((cols, cols), 1)
    earlier = one_hot((r < c) & (jnp.floor(r / span) == jnp.floor(c / span)))
    ahead = dot(named.astype(BF16), earlier)
    return jnp.where(named > 0, ahead, -1.0), weight


def fill_pick(pick, seat, per_expert, blocks, span):
    total, cols = pick.shape
    rows = seat.shape[0]
    part = total // SIDE
    seat16 = seat.astype(BF16)
    column = 16.0 * jnp.floor(iota((part, cols), 1) / span)
    for p in range(SIDE):
        at = iota((part, rows), 0) + float(p * part)
        spread = one_hot(jnp.floor((at + 0.5) / per_expert) == iota((part, rows), 1))
        slot = iota((part, 1), 0) + float(p * part)
        ten = jnp.floor((slot + 0.5) / MOST)
        code = (slot - MOST * ten) + 16.0 * (ten - blocks * jnp.floor((ten + 0.5) / blocks))
        pick[p * part : (p + 1) * part, :] = one_hot(dot(spread, seat16) + column == code)


def fill_mix(mix, seat, weight, per_expert, blocks, span):
    cols, total = mix.shape
    rows = seat.shape[0]
    both = jnp.concatenate([seat, weight, jnp.zeros((LANES - 2 * rows, cols), F32)], axis=0)
    turned = jnp.transpose(both).astype(BF16)
    owner = jnp.floor((iota((LANES, total), 1) + 0.5) / per_expert)
    lane = iota((LANES, total), 0)
    spread_seat = one_hot(owner == lane)
    spread_mix = one_hot(owner + float(rows) == lane)
    slot = iota((1, total), 1)
    ten = jnp.floor((slot + 0.5) / MOST)
    code = (slot - MOST * ten) + 16.0 * (ten - blocks * jnp.floor((ten + 0.5) / blocks))
    part = cols // SIDE
    for p in range(SIDE):
        here = turned[p * part : (p + 1) * part, :]
        row = 16.0 * jnp.floor((iota((part, 1), 0) + float(p * part)) / span)
        mix[p * part : (p + 1) * part, :] = jnp.where(
            dot(here, spread_seat) + row == code, dot(here, spread_mix), 0.0
        ).astype(BF16)


def fill_swap(swap, outer, inner):
    total = swap.shape[0]
    part = total // SIDE
    lane = iota((part, total), 1)
    for p in range(SIDE):
        slot = iota((part, 1), 0) + float(p * part)
        ten = jnp.floor((slot + 0.5) / MOST)
        o = jnp.floor((ten + 0.5) / inner)
        i = ten - o * inner
        swap[p * part : (p + 1) * part, :] = one_hot(lane == (i * outer + o) * MOST + (slot - MOST * ten))


def read_info(info):
    ids = []
    mixes = []
    for k in range(TOP_K):
        inside = info[k : k + 1, :]
        group = info[2 * TOP_K + k // 2 : 2 * TOP_K + k // 2 + 1, :]
        ids.append(jnp.where(inside >= 0, inside + float(SIDE * SIDE) * group, -1.0))
        mixes.append(info[TOP_K + k : TOP_K + k + 1, :])
    return ids, mixes


def dispatch_kernel(
    groups, slots,
    aff_ref, gid_ref, eid_ref, tok_ref, wg_ref, wu_ref,
    hid_ref, mix_g, mix_x, mix_z, back_ref,
    info_out, info_x, info_z, meta_out, meta_in, first_out, first_in, wide_x, wide_z,
    out_g, relay_g, y_out, y_in, rows, acc_g, acc_u, wbuf_g, wbuf_u, pick_g, pick_x, pick_z, swap, sel, stage, table,
    s_info, r_info, s_meta, r_meta, s_first, r_first, s_wide_x, s_wide_z, r_wide, s_one, r_one,
    s_two, s_y, r_y, s_end, r_rows, w_sem, mix_sem,
):
    g, z, x = position()
    barrier_signal(g, z, x, groups)
    tok = tok_ref.shape[0]
    width = tok_ref.shape[1] // CHUNKS
    seats = tok * TOPG // groups
    held = groups * seats
    block = SIDE * slots
    total = SIDE * block
    local = SIDE * SIDE

    def columns(c):
        return pl.ds(pl.multiple_of(c * width, width), width)

    def group_at_step(t):
        return jnp.minimum(2 * t, t + 2)

    def step_column(t):
        return jnp.minimum(4 * t, 3 * t + 2)

    def group_column(k):
        return k // 2 * 4 + k % 2 + 2 * (k // 5)

    def weights(c):
        slot = lax.rem(c, 2)
        return (
            pltpu.make_async_copy(wg_ref.at[columns(c)], wbuf_g.at[slot], w_sem.at[0, slot]),
            pltpu.make_async_copy(wu_ref.at[columns(c)], wbuf_u.at[slot], w_sem.at[1, slot]),
        )

    for c in range(2):
        for cp in weights(c):
            cp.start()

    aff = aff_ref[...]
    scaled = (2.5 * aff / jnp.sum(aff, axis=0, keepdims=True)).astype(BF16).astype(F32)
    gid = gid_ref[...].astype(F32)
    eid = eid_ref[...].astype(F32)
    owner = jnp.floor(eid / float(local))
    chosen = jnp.concatenate([gid[k // 2 : k // 2 + 1, :] for k in range(TOP_K)], axis=0)
    is_valid = owner == chosen
    mixing = jnp.where(is_valid, scaled, 0.0)
    inside = jnp.where(is_valid, eid - float(local) * owner, -1.0)
    rt_t = jnp.concatenate(
        [inside, mixing, gid, jnp.zeros((LANES - 2 * TOP_K - TOPG, tok), F32)], axis=0
    )
    rt = jnp.transpose(rt_t)
    info_out[...] = rt.astype(BF16)
    info_x[x] = info_out[...]
    info_z[z] = info_out[...]

    barrier_wait(groups)
    for step in (2, 1, 3):
        peer = ring(x, step)
        remote(info_out, info_x.at[x], s_info.at[0], r_info.at[0], g, z, peer)
        peer = ring(z, step)
        remote(info_out, info_z.at[z], s_info.at[1], r_info.at[1], g, peer, x)

    group_at = iota((groups, tok), 0)
    member = jnp.zeros((groups, tok), F32)
    for j in range(TOPG):
        member = member + jnp.where(rt_t[2 * TOP_K + j : 2 * TOP_K + j + 1, :] == group_at, 1.0, 0.0)
    earlier = one_hot(iota((tok, tok), 0) < iota((tok, tok), 1))
    seat = jnp.where(member > 0, dot(member.astype(BF16), earlier), -1.0)
    seat_at = iota((seats, tok), 0)
    for gg in range(groups):
        sel[gg * seats : (gg + 1) * seats, :] = one_hot(seat_at == seat[gg : gg + 1, :])
    meta_out[0] = dot(sel[...], info_out[...]).astype(BF16).reshape(groups, seats, LANES)
    send_groups(meta_out, meta_in, 0, g, z, x, groups, s_meta, r_meta)

    def first(t, carry):
        got = dot(sel[...], tok_ref[:, columns(group_column(t))]).astype(BF16)
        first_out[t] = got.reshape(groups, seats, width)
        send_groups(first_out, first_in, t, g, z, x, groups, s_first, r_first.at[t])

        @pl.when(t < N_X)
        def _():
            wide_x[t, x] = tok_ref[:, columns(step_column(t + 1) - 2)]
            for step in (2, 1, 3):
                remote(wide_x.at[t, x], wide_x.at[t, x], s_wide_x, r_wide.at[t], g, z, ring(x, step))
            wide_z[t, z] = tok_ref[:, columns(step_column(t + 1) - 1)]
            for step in (2, 1, 3):
                remote(wide_z.at[t, z], wide_z.at[t, z], s_wide_z, r_wide.at[N_X + t], g, ring(z, step), x)

        return carry

    lax.fori_loop(0, N_G, first, 0)

    def clear(b, carry):
        at = pl.ds(pl.multiple_of(b * slots, slots), slots)
        acc_g[at, :] = jnp.zeros((slots, acc_g.shape[1]), F32)
        acc_u[at, :] = jnp.zeros((slots, acc_u.shape[1]), F32)
        return carry

    lax.fori_loop(0, total // slots, clear, 0)

    def plan_g():
        wait_bytes(meta_in.at[0, pl.ds(0, groups - 1)], r_meta)
        ids, mixes = read_info(jnp.transpose(meta_in[0].reshape(held, LANES).astype(F32)))
        own = iota((local, held), 0) + float(local) * g.astype(F32)
        seat_in, weight = rank_table(ids, mixes, own, float(seats))
        fill_pick(pick_g, seat_in, float(slots), float(groups), float(seats))
        table[0, 0:local, :] = seat_in
        table[0, local : 2 * local, :] = weight

    def plan_wide(info, which, own, pick):
        wait_bytes(info.at[pl.ds(0, SIDE - 1)], r_info.at[which])
        ids, mixes = read_info(jnp.transpose(info[...].reshape(held, LANES).astype(F32)))
        seat_in, weight = rank_table(ids, mixes, own, float(tok))
        fill_pick(pick, seat_in, float(SIDE * MOST), float(SIDE), float(tok))
        table[1 + which, 0 : 2 * local, :] = seat_in
        table[1 + which, 2 * local : 4 * local, :] = weight

    def plan_x():
        plan_wide(info_x, 0, iota((2 * local, held), 0) * float(SIDE) + x.astype(F32), pick_x)

    def plan_z():
        row = iota((2 * local, held), 0)
        own = jnp.floor(row / float(SIDE)) * float(local - SIDE) + row + float(SIDE) * z.astype(F32)
        plan_wide(info_z, 1, own, pick_z)

    plan_g()

    def to_peers(c, src, pick):
        for p in range(SIDE):
            got = dot(pick[p * block : (p + 1) * block, :], src).astype(BF16)
            y_out[c, pl.ds(p * SIDE, SIDE)] = got.reshape(SIDE, slots, width)
        send_pairs(y_out, y_in, c, g, z, x, groups, s_y.at[c], r_y.at[c])

    def reorder(c):
        wait_bytes(y_in.at[c, pl.ds(0, 2 * groups - 2)], r_y.at[c])
        wait_bytes(y_out.at[c, pl.ds(0, 2 * groups - 2)], s_y.at[c])
        src = y_in[c].reshape(total, width)
        for p in range(SIDE):
            got = dot(swap[p * block : (p + 1) * block, :], src).astype(BF16)
            y_out[c, pl.ds(p * SIDE, SIDE)] = got.reshape(SIDE, slots, width)

    def step(t, carry):
        def spread_group(k, inner):
            wait_bytes(first_in.at[k, pl.ds(0, groups - 1)], r_first.at[k])
            src = first_in[k].reshape(held, width)
            for p in range(SIDE):
                got = dot(pick_g[p * block : (p + 1) * block, :], src).astype(BF16)
                out_g[k, p] = got.reshape(SIDE, slots, width)

            @pl.when(lax.rem(k, 2) == 0)
            def _():
                along_x(out_g, k, relay_g, k, g, z, x, s_one, r_one.at[k])

            @pl.when(lax.rem(k, 2) == 1)
            def _():
                along_z(out_g, k, relay_g, k, g, z, x, s_one, r_one.at[k])

            return inner

        @pl.when(t < N_X)
        def _():
            lax.fori_loop(group_at_step(t), group_at_step(t + 1), spread_group, 0)

        pl.when(t == 0)(plan_x)

        @pl.when(t < N_X)
        def _():
            wait_bytes(wide_x.at[t, pl.ds(0, SIDE - 1)], r_wide.at[t])
            to_peers(t, wide_x[t].reshape(held, width), pick_x)

        pl.when(t == 0)(plan_z)

        @pl.when(t < N_Z)
        def _():
            wait_bytes(wide_z.at[t, pl.ds(0, SIDE - 1)], r_wide.at[N_X + t])
            to_peers(N_X + t, wide_z[t].reshape(held, width), pick_z)

        @pl.when(t == 0)
        def _():
            fill_swap(swap, local, groups)

        def pass_group(k, inner):
            wait_bytes(relay_g.at[k, pl.ds(0, SIDE - 1)], r_one.at[k])

            @pl.when(lax.rem(k, 2) == 0)
            def _():
                along_z(relay_g, k, rows, group_column(k), g, z, x, s_two, r_rows.at[group_column(k)])

            @pl.when(lax.rem(k, 2) == 1)
            def _():
                along_x(relay_g, k, rows, group_column(k), g, z, x, s_two, r_rows.at[group_column(k)])

            return inner

        @pl.when((t >= 1) & (t < N_X + 1))
        def _():
            lax.fori_loop(group_at_step(t - 1), group_at_step(t), pass_group, 0)

        @pl.when((t >= 1) & (t < N_X + 1))
        def _():
            c = t - 1
            reorder(c)
            for step in (2, 1, 3):
                peer = ring(z, step)
                remote(
                    y_out.at[c, pl.ds(SIDE * peer, SIDE)], rows.at[step_column(t) - 2, z], s_end, r_rows.at[step_column(t) - 2],
                    g, peer, x,
                )
            rows[step_column(t) - 2, z] = y_out[c, pl.ds(SIDE * z, SIDE)]

        @pl.when((t >= 1) & (t < N_Z + 1))
        def _():
            c = t - 1
            reorder(N_X + c)
            for step in (2, 1, 3):
                peer = ring(x, step)
                remote(
                    y_out.at[N_X + c, pl.ds(SIDE * peer, SIDE)], rows.at[step_column(t) - 1, :, x], s_end,
                    r_rows.at[step_column(t) - 1], g, z, peer,
                )
            for p in range(SIDE):
                rows[step_column(t) - 1, p, x] = y_out[N_X + c, SIDE * x + p]

        @pl.when(t == 1)
        def _():
            def keep(mix):
                put = pltpu.make_async_copy(stage, mix, mix_sem)
                put.start()
                put.wait()

            fill_mix(stage, table[0, 0:local, :], table[0, local : 2 * local, :], float(slots), float(groups), float(seats))
            keep(mix_g)
            fill_mix(stage, table[1, 0 : 2 * local, :], table[1, 2 * local : 4 * local, :], float(SIDE * MOST), float(SIDE), float(tok))
            keep(mix_x)
            fill_mix(stage, table[2, 0 : 2 * local, :], table[2, 2 * local : 4 * local, :], float(SIDE * MOST), float(SIDE), float(tok))
            keep(mix_z)
            seat_t = jnp.transpose(jnp.concatenate([seat, jnp.full((tok - groups, tok), -1.0, F32)], axis=0))
            lane_at = iota((tok, held), 1)
            back = jnp.zeros((tok, held), F32)
            for gg in range(groups):
                column = seat_t[:, gg : gg + 1]
                want = jnp.where(column >= 0, column + float(gg * seats), -1.0)
                back = back + jnp.where(lane_at == want, 1.0, 0.0)
            back_ref[...] = back.astype(BF16)

        def multiply(c, carry_in):
            slot = lax.rem(c, 2)
            wait_bytes(rows.at[c, pl.ds(0, SIDE - 1)], r_rows.at[c])
            for cp in weights(c):
                cp.wait()

            def piece(p, inner):
                at = pl.ds(pl.multiple_of(p * block, block), block)
                part = rows[c, p].reshape(block, width)
                acc_g[at, :] += dot(part, wbuf_g[slot])
                acc_u[at, :] += dot(part, wbuf_u[slot])
                return inner

            lax.fori_loop(0, SIDE, piece, 0)

            @pl.when(c + 2 < CHUNKS)
            def _():
                for cp in weights(c + 2):
                    cp.start()

            return carry_in

        @pl.when(t >= 2)
        def _():
            c = t - 2
            lax.fori_loop(step_column(c), step_column(c + 1), multiply, 0)

        return carry

    lax.fori_loop(0, N_X + 2, step, 0)

    def finish(b, carry):
        at = pl.ds(pl.multiple_of(b * slots, slots), slots)
        v = acc_g[at, :]
        hid_ref[at, :] = (v / (1.0 + jnp.exp(-v)) * acc_u[at, :]).astype(BF16)
        return carry

    lax.fori_loop(0, total // slots, finish, 0)
    wait_bytes(info_x.at[pl.ds(0, SIDE - 1)], s_info.at[0])
    wait_bytes(info_z.at[pl.ds(0, SIDE - 1)], s_info.at[1])
    wait_bytes(meta_out.at[0, pl.ds(0, groups - 1)], s_meta)
    wait_bytes(first_out.at[:, pl.ds(0, groups - 1)], s_first)
    wait_bytes(wide_x.at[:, pl.ds(0, SIDE - 1)], s_wide_x)
    wait_bytes(wide_z.at[:, pl.ds(0, SIDE - 1)], s_wide_z)
    wait_bytes(out_g.at[:, pl.ds(0, SIDE - 1)], s_one)
    wait_bytes(relay_g.at[:, pl.ds(0, SIDE - 1)], s_two)
    wait_bytes(y_out.at[:, pl.ds(0, SIDE * (SIDE - 1))], s_end)


def return_kernel(
    groups, slots,
    hid_ref, mix_hbm_g, mix_hbm_x, mix_hbm_z, back_ref, wd_ref,
    out_ref,
    out_buf, relay_g, rows_g, mid, y_out, y_in, part_out, part_in, sum_out, sum_in, wbuf, swap, mix_g, mix_x, mix_z,
    s_one, r_one, s_two, r_two, s_mid, r_mid, s_y, r_y, s_last, r_last, s_sum_x, s_sum_z, r_sum, w_sem, mix_sem,
):
    g, z, x = position()
    barrier_signal(g, z, x, groups)
    tok = out_ref.shape[0]
    width = out_ref.shape[1] // CHUNKS
    held = mix_g.shape[0]
    seats = held // groups
    block = SIDE * slots
    total = SIDE * block

    def columns(c):
        return pl.ds(pl.multiple_of(c * width, width), width)

    def group_at_step(t):
        return jnp.maximum(jnp.minimum(2 * t - 1, t + 2), 0)

    def step_column(t):
        return 2 * t + group_at_step(t)

    def group_column(k):
        return 2 * ((k + 1) // 2) + 2 + k

    def weights(c):
        slot = lax.rem(c, 2)
        return pltpu.make_async_copy(wd_ref.at[:, columns(c)], wbuf.at[slot], w_sem.at[slot])

    for c in range(2):
        weights(c).start()
    mixes = [
        pltpu.make_async_copy(mix_hbm_g, mix_g, mix_sem.at[0]),
        pltpu.make_async_copy(mix_hbm_x, mix_x, mix_sem.at[1]),
        pltpu.make_async_copy(mix_hbm_z, mix_z, mix_sem.at[2]),
    ]

    def down(c):
        slot = lax.rem(c, 2)
        weights(c).wait()

        def piece(p, inner):
            at = pl.ds(pl.multiple_of(p * block, block), block)
            got = dot(hid_ref[at, :], wbuf[slot]).astype(BF16)
            out_buf[c, p] = got.reshape(SIDE, slots, width)
            return inner

        lax.fori_loop(0, SIDE, piece, 0)

        @pl.when(c + 2 < CHUNKS)
        def _():
            weights(c + 2).start()

    down(0)
    barrier_wait(groups)

    def to_sources(c):
        wait_bytes(mid.at[c, pl.ds(0, SIDE * (SIDE - 1))], r_mid.at[c])
        src = mid[c].reshape(total, width)
        for p in range(SIDE):
            got = dot(swap[p * block : (p + 1) * block, :], src).astype(BF16)
            y_out[c, pl.ds(p * SIDE, SIDE)] = got.reshape(SIDE, slots, width)
        send_pairs(y_out, y_in, c, g, z, x, groups, s_y, r_y.at[c])

    def weigh(c, mix):
        wait_bytes(y_in.at[c, pl.ds(0, 2 * groups - 2)], r_y.at[c])
        got = dot(mix[...], y_in[c].reshape(total, width)).astype(BF16)
        sum_out[c] = got.reshape(SIDE, tok, width)

    def add_up(c):
        wait_bytes(sum_in.at[c, pl.ds(0, SIDE - 1)], r_sum.at[c])
        got = sum_in[c, 0].astype(F32)
        for b in range(1, SIDE):
            got = got + sum_in[c, b].astype(F32)
        return got.astype(BF16)

    def step(t, carry):
        @pl.when(t < N_X)
        def _():
            c = step_column(t)

            @pl.when(t > 0)
            def _():
                down(c)

            for step in (2, 1, 3):
                peer = ring(z, step)
                remote(out_buf.at[c, peer], mid.at[t, pl.ds(SIDE * z, SIDE)], s_mid.at[0], r_mid.at[t], g, peer, x)
            mid[t, pl.ds(SIDE * z, SIDE)] = out_buf[c, z]

        @pl.when(t < N_Z)
        def _():
            c = step_column(t) + 1
            down(c)
            for step in (2, 1, 3):
                peer = ring(x, step)
                remote(
                    out_buf.at[c, :, peer], mid.at[N_X + t, pl.ds(SIDE * x, SIDE)], s_mid.at[1],
                    r_mid.at[N_X + t], g, z, peer,
                )
            for p in range(SIDE):
                mid[N_X + t, SIDE * x + p] = out_buf[c, p, x]

        def start_group(k, inner):
            c = group_column(k)
            down(c)

            @pl.when(lax.rem(k, 2) == 0)
            def _():
                along_x(out_buf, c, relay_g, k, g, z, x, s_one, r_one.at[k])

            @pl.when(lax.rem(k, 2) == 1)
            def _():
                along_z(out_buf, c, relay_g, k, g, z, x, s_one, r_one.at[k])

            return inner

        @pl.when(t < N_X)
        def _():
            lax.fori_loop(group_at_step(t), group_at_step(t + 1), start_group, 0)

        @pl.when(t == 0)
        def _():
            for cp in mixes:
                cp.start()
            fill_swap(swap, groups, SIDE * SIDE)
            for cp in mixes:
                cp.wait()

        @pl.when((t >= 1) & (t < N_X + 1))
        def _():
            to_sources(t - 1)

        @pl.when((t >= 1) & (t < N_Z + 1))
        def _():
            to_sources(N_X + t - 1)

        def pass_group(k, inner):
            wait_bytes(relay_g.at[k, pl.ds(0, SIDE - 1)], r_one.at[k])

            @pl.when(lax.rem(k, 2) == 0)
            def _():
                along_z(relay_g, k, rows_g, k, g, z, x, s_two, r_two.at[k])

            @pl.when(lax.rem(k, 2) == 1)
            def _():
                along_x(relay_g, k, rows_g, k, g, z, x, s_two, r_two.at[k])

            return inner

        @pl.when((t >= 1) & (t < N_X + 1))
        def _():
            lax.fori_loop(group_at_step(t - 1), group_at_step(t), pass_group, 0)

        @pl.when((t >= 2) & (t < N_X + 2))
        def _():
            c = t - 2
            weigh(c, mix_x)
            for step in (2, 1, 3):
                peer = ring(x, step)
                remote(sum_out.at[c, peer], sum_in.at[c, x], s_sum_x, r_sum.at[c], g, z, peer)
            sum_in[c, x] = sum_out[c, x]

        @pl.when((t >= 2) & (t < N_Z + 2))
        def _():
            c = N_X + t - 2
            weigh(c, mix_z)
            for step in (2, 1, 3):
                peer = ring(z, step)
                remote(sum_out.at[c, peer], sum_in.at[c, z], s_sum_z, r_sum.at[c], g, peer, x)
            sum_in[c, z] = sum_out[c, z]

        def weigh_group(k, inner):
            wait_bytes(rows_g.at[k, pl.ds(0, SIDE - 1)], r_two.at[k])
            got = dot(mix_g[...], rows_g[k].reshape(total, width)).astype(BF16)
            part_out[k] = got.reshape(groups, seats, width)
            send_groups(part_out, part_in, k, g, z, x, groups, s_last, r_last.at[k])
            return inner

        @pl.when((t >= 2) & (t < N_X + 2))
        def _():
            lax.fori_loop(group_at_step(t - 2), group_at_step(t - 1), weigh_group, 0)

        def place_group(k, inner):
            wait_bytes(part_in.at[k, pl.ds(0, groups - 1)], r_last.at[k])
            out_ref[:, columns(group_column(k))] = dot(back_ref[...], part_in[k].reshape(held, width)).astype(BF16)
            return inner

        @pl.when((t >= 3) & (t < N_X + 3))
        def _():
            lax.fori_loop(group_at_step(t - 3), group_at_step(t - 2), place_group, 0)

        @pl.when((t >= 3) & (t < N_X + 3))
        def _():
            out_ref[:, columns(step_column(t - 3))] = add_up(t - 3)

        @pl.when((t >= 3) & (t < N_Z + 3))
        def _():
            out_ref[:, columns(step_column(t - 3) + 1)] = add_up(N_X + t - 3)

        return carry

    lax.fori_loop(0, N_X + 3, step, 0)
    wait_bytes(relay_g.at[:, pl.ds(0, SIDE - 1)], s_one)
    wait_bytes(rows_g.at[:, pl.ds(0, SIDE - 1)], s_two)
    wait_bytes(mid.at[pl.ds(0, N_X), pl.ds(0, SIDE * (SIDE - 1))], s_mid.at[0])
    wait_bytes(mid.at[pl.ds(N_X, N_Z), pl.ds(0, SIDE * (SIDE - 1))], s_mid.at[1])
    wait_bytes(y_out.at[:, pl.ds(0, 2 * groups - 2)], s_y)
    wait_bytes(part_out.at[:, pl.ds(0, groups - 1)], s_last)
    wait_bytes(sum_out.at[pl.ds(0, N_X), pl.ds(0, SIDE - 1)], s_sum_x)
    wait_bytes(sum_out.at[pl.ds(N_X, N_Z), pl.ds(0, SIDE - 1)], s_sum_z)


def shards(hidden_states, affinity, group_ids, expert_ids, w_gate, w_up, w_down):
    tok, model = hidden_states.shape
    hid = w_gate.shape[2]
    groups = lax.axis_size("group")
    slots = MOST * groups
    seats = tok * TOPG // groups
    held = groups * seats
    total = SIDE * SIDE * slots
    width = model // CHUNKS
    wide = N_X + N_Z

    vmem = pl.BlockSpec(memory_space=pltpu.VMEM)
    anywhere = pl.BlockSpec(memory_space=pl.ANY)
    dma = pltpu.SemaphoreType.DMA

    def grid4(n):
        return pltpu.VMEM((n, SIDE, SIDE, slots, width), BF16)

    def pairs(n):
        return pltpu.VMEM((n, SIDE * SIDE, slots, width), BF16)

    def seated(n, w):
        return pltpu.VMEM((n, groups, seats, w), BF16)

    def spread(n):
        return pltpu.VMEM((n, SIDE, tok, width), BF16)

    mix_shape = jax.ShapeDtypeStruct((held, total), BF16)
    hidden, mix_g, mix_x, mix_z, back = pl.pallas_call(
        functools.partial(dispatch_kernel, groups, slots),
        out_shape=(
            jax.ShapeDtypeStruct((total, hid), BF16), mix_shape, mix_shape, mix_shape,
            jax.ShapeDtypeStruct((tok, held), BF16),
        ),
        in_specs=[vmem, vmem, vmem, vmem, anywhere, anywhere],
        out_specs=(vmem, anywhere, anywhere, anywhere, vmem),
        scratch_shapes=[
            pltpu.VMEM((tok, LANES), BF16),
            pltpu.VMEM((SIDE, tok, LANES), BF16),
            pltpu.VMEM((SIDE, tok, LANES), BF16),
            seated(1, LANES), seated(1, LANES),
            seated(N_G, width), seated(N_G, width),
            spread(N_X), spread(N_Z),
            grid4(N_G), grid4(N_G),
            pairs(wide), pairs(wide),
            grid4(CHUNKS),
            pltpu.VMEM((total, hid), F32),
            pltpu.VMEM((total, hid), F32),
            pltpu.VMEM((2, width, hid), BF16),
            pltpu.VMEM((2, width, hid), BF16),
            pltpu.VMEM((total, held), BF16),
            pltpu.VMEM((total, held), BF16),
            pltpu.VMEM((total, held), BF16),
            pltpu.VMEM((total, total), BF16),
            pltpu.VMEM((held, tok), BF16),
            pltpu.VMEM((held, total), BF16),
            pltpu.VMEM((3, LANES, held), F32),
            dma((2,)), dma((2,)), dma, dma, dma, dma((N_G,)), dma, dma, dma((wide,)), dma, dma((N_G,)),
            dma, dma((wide,)), dma((wide,)), dma, dma((CHUNKS,)), dma((2, 2)), dma,
        ],
        compiler_params=pltpu.CompilerParams(
            collective_id=0, has_side_effects=True, vmem_limit_bytes=63 * 2**20
        ),
        name="dispatch",
    )(affinity.T, group_ids.T, expert_ids.T, hidden_states, w_gate[0], w_up[0])

    return pl.pallas_call(
        functools.partial(return_kernel, groups, slots),
        out_shape=jax.ShapeDtypeStruct((tok, model), BF16),
        in_specs=[vmem, anywhere, anywhere, anywhere, vmem, anywhere],
        out_specs=vmem,
        scratch_shapes=[
            grid4(CHUNKS), grid4(N_G), grid4(N_G),
            pairs(wide), pairs(wide), pairs(wide),
            seated(N_G, width), seated(N_G, width),
            spread(wide), spread(wide),
            pltpu.VMEM((2, hid, width), BF16),
            pltpu.VMEM((total, total), BF16),
            pltpu.VMEM((held, total), BF16),
            pltpu.VMEM((held, total), BF16),
            pltpu.VMEM((held, total), BF16),
            dma, dma((N_G,)), dma, dma((N_G,)), dma((2,)), dma((wide,)), dma, dma((wide,)),
            dma, dma((N_G,)), dma, dma, dma((wide,)), dma((2,)), dma((3,)),
        ],
        compiler_params=pltpu.CompilerParams(
            collective_id=1, has_side_effects=True, vmem_limit_bytes=60 * 2**20
        ),
        name="giveback",
    )(hidden, mix_g, mix_x, mix_z, back, w_down[0])


def solution(mesh):
    placed = (
        P(("group", "local"), None),
        P(("group", "local"), None),
        P(("group", "local"), None),
        P(("group", "local"), None),
        P(("group", "local"), None, None),
        P(("group", "local"), None, None),
        P(("group", "local"), None, None),
    )
    return jax.shard_map(
        shards, mesh=mesh, in_specs=placed, out_specs=P(("group", "local"), None), check_vma=False
    )
```
